32 devices in a mesh: grp: 2 (over y), tm: 4 (over z), spin: 2 (over core), rows: 2 (over x).
Axes of the slice: x: 2, y: 2, z: 4, core: 2. Of those that a mesh axis runs over, the one named last changes fastest.
Arguments:
- ising_field: int32 [32, 768], P(('grp', 'tm')), parts along dimension 0, may hold values from 0 to 1
- bond_sites: int32 [3072, 2], replicated, may hold values from 0 to 767
- hopping: float32 [3072], replicated, may hold values from 0.5 to 2
- tile_cols: int32 [6, 3], replicated, may hold values from 0 to 5, as said below
Outputs:
- xcorr: float32 [2, 8, 768, 768], P('spin', ('grp', 'tm'), None, 'rows'), parts along dimension 1
The draws below stay inside these ranges and needn't reach their ends.
There are 2 independent parts, one for each index of `grp`. The reference program is written for one: setup_inputs(seed, part) draws one part's arguments, and reference() takes and returns one part's arrays. A program takes and returns all parts, laid end to end along the dimension named above; an argument that names none is the same for every part. Nothing has to cross between parts.
Inputs may be any that keep to these rules, and one draw needn't show every extreme that they name: `ising_field`: 0 stands for the field value -1 and 1 for +1. `bond_sites`: A bond whose tile pair is not in tile_cols adds nothing to H, because tile_mask removes it; its entry in `hopping` is not zero. `tile_cols`: row r lists r first and then the two tiles beside r on a cycle through all 6 tiles drawn from the seed, so each tile row names 3 distinct tiles and the pattern is symmetric.
All inputs are finite; a program needn't handle non-finite values.
Results may differ from the reference program's by a relative error of at most 0.0003.
Values sent between devices are 32-bit elements; how exact they have to be, the bound alone decides.
No kernel may reach another device: no remote copies, remote signals or barrier semaphores. Data moves between devices by JAX's collectives and lax.ppermute only.
A program may use at most 64 MiB of HBM per device.

```python
import math
import jax
import jax.numpy as jnp
from jax import lax

N = 768
NT = 6
BONDS = 3072
SL_DEV = 4
SLICES = 16
BLOCKS = 4


def draw_tile_cols(key, part):
    ordering = jax.random.permutation(key, NT).astype(jnp.int32)
    position = jnp.zeros((NT,), jnp.int32).at[ordering].set(jnp.arange(NT, dtype=jnp.int32))
    following = ordering[(position + 1) % NT]
    preceding = ordering[(position - 1 + NT) % NT]
    return jnp.stack([jnp.arange(NT, dtype=jnp.int32), following, preceding], axis=1).astype(jnp.int32)


def with_ends(array, own_key, smallest, largest):
    spot = [jax.random.randint(jax.random.fold_in(own_key, axis), (), 0, length) for axis, length in enumerate(array.shape)]
    longest = array.shape.index(max(array.shape))
    neighbour = spot[:longest] + [(spot[longest] + 1) % array.shape[longest]] + spot[longest + 1:]
    return array.at[tuple(spot)].set(smallest).at[tuple(neighbour)].set(largest)


def setup_inputs(seed: int = 0, part: int = 0) -> dict:
    key_list = jax.random.split(jax.random.key(seed), 5)
    own_keys = jax.random.split(jax.random.fold_in(key_list[4], part), 5)
    return {
        "ising_field": with_ends(jax.random.randint(own_keys[0], (SLICES, N), 0, 2), jax.random.fold_in(own_keys[0], 1), 0, 1).astype(jnp.int32),
        "bond_sites": with_ends(jax.random.randint(key_list[1], (BONDS, 2), 0, N), jax.random.fold_in(key_list[1], 1), 0, N - 1).astype(jnp.int32),
        "hopping": jnp.clip(jnp.exp(jax.random.uniform(key_list[2], (BONDS,), jnp.float32, math.log(0.5), math.log(2.0))), 0.5, 2.0),
        "tile_cols": draw_tile_cols(jax.random.fold_in(key_list[4], 71), part),
    }


def matmul_hi(left, right):
    return jnp.dot(left.astype(jnp.float32), right.astype(jnp.float32), precision=lax.Precision.HIGHEST, preferred_element_type=jnp.float32)

def build_kinetic(bond_sites, hopping, tile_cols, matrix_order, hop_scale):
    n_tiles = tile_cols.shape[0]
    tile_len = matrix_order // n_tiles
    tile_mask = jnp.any(tile_cols[:, :, None] == jnp.arange(n_tiles, dtype=jnp.int32)[None, None, :], axis=1).astype(jnp.float32)
    site_from = bond_sites[:, 0]
    site_to = bond_sites[:, 1]
    kept_mask = tile_mask[site_from // tile_len, site_to // tile_len]
    weights = hopping * kept_mask
    hop_matrix = jnp.zeros((matrix_order, matrix_order), jnp.float32)
    hop_matrix = hop_matrix.at[site_from, site_to].add(weights).at[site_to, site_from].add(weights)
    return jnp.eye(matrix_order, dtype=jnp.float32) + hop_scale * hop_matrix

def reference(ising_field, bond_sites, hopping, tile_cols):
    kinetic = build_kinetic(bond_sites, hopping, tile_cols, N, 0.5 / SLICES)
    coupling = 1.5 / math.sqrt(SLICES)
    spins_pm = (2 * ising_field - 1).astype(jnp.float32)
    identity = jnp.eye(N, dtype=jnp.float32)
    greens = []
    for spin_sign in (1.0, -1.0):
        factors = jnp.exp(spin_sign * coupling * spins_pm).reshape(BLOCKS, SL_DEV, N)

        def cluster_of(block_factors):

            def apply_slice(carry, slice_factors):
                return (slice_factors[:, None] * matmul_hi(kinetic, carry), None)
            result, _ = lax.scan(apply_slice, identity, block_factors)
            return result
        clusters = lax.map(cluster_of, factors)

        def cyclic_of(start):

            def apply_block(offset_step, carry):
                return matmul_hi(clusters[(start + offset_step) % BLOCKS], carry)
            return lax.fori_loop(0, BLOCKS, apply_block, identity)
        products = lax.map(cyclic_of, jnp.arange(BLOCKS, dtype=jnp.int32))

        def green_of(product):
            col_max = jnp.max(lax.optimization_barrier(jnp.sum(product, axis=0)))
            power = product / (2.0 * col_max)
            return jnp.linalg.solve(identity + power, identity)
        greens.append(lax.map(green_of, products))
    green_up, green_down = greens
    first = green_up * (identity - jnp.swapaxes(green_down, 1, 2))
    second = green_down * (identity - jnp.swapaxes(green_up, 1, 2))
    return jnp.stack([first, second])
```

```python
import functools
import math

import jax
import jax.numpy as jnp
from jax import lax
from jax.experimental import pallas as pl
from jax.experimental.pallas import tpu as pltpu
from jax.sharding import PartitionSpec as P

F32 = jnp.float32
BF16 = jnp.bfloat16


def dot(left, right):
    return jnp.dot(left, right, preferred_element_type=F32)


def split(x):
    high = x.astype(BF16)
    return high, (x - high.astype(F32)).astype(BF16)


def cycle_order(tile_cols_ref, n_tiles):
    order = [jnp.int32(0), tile_cols_ref[0, 1]]
    while len(order) < n_tiles:
        before, here = order[-2], order[-1]
        one, two = tile_cols_ref[here, 1], tile_cols_ref[here, 2]
        order.append(jnp.where(one == before, two, one))
    return order


def tile_ds(tile, tile_len):
    return pl.ds(pl.multiple_of(tile * tile_len, tile_len), tile_len)


def kinetic_kernel(n_tiles, tile_len, scale, tile_cols_ref, sites_ref, hopping_ref, weight_ref, acc_ref):
    order = cycle_order(tile_cols_ref, n_tiles)
    shift = tile_len.bit_length() - 1
    bonds = sites_ref.shape[1]
    pair_len = 2 * tile_len
    chunk = min(bonds, 512)

    def position(site):
        tile = site >> shift
        place = jnp.zeros_like(site)
        for p in range(1, n_tiles):
            place = jnp.where(tile == order[p], p, place)
        return place, place * tile_len + (site & (tile_len - 1))

    acc_ref[...] = jnp.zeros_like(acc_ref)

    def add_bonds(step, carry):
        lanes = pl.ds(pl.multiple_of(step * chunk, chunk), chunk)
        tile_a, site_a = position(sites_ref[0:1, lanes])
        tile_b, site_b = position(sites_ref[1:2, lanes])
        apart = jnp.abs(tile_a - tile_b)
        kept = (apart <= 1) | (apart == n_tiles - 1)
        weight = jnp.where(kept, hopping_ref[0:1, lanes] * scale, 0.0)
        weight_high = weight.astype(BF16).astype(F32)
        weight_low = weight - weight_high
        swap = ((tile_a >> 1) != (tile_b >> 1)) & ((tile_a & 1) == 0)
        first = jnp.where(swap, site_b, site_a)
        second = jnp.where(swap, site_a, site_b)
        row_ids = lax.broadcasted_iota(jnp.int32, (tile_len, chunk), 0)
        rows_of, high_of, low_of = [], [], []
        for p in range(n_tiles):
            ids = row_ids + p * tile_len
            rows_of.append(jnp.where(first == ids, 1.0, 0.0).astype(BF16))
            hit = second == ids
            high_of.append(jnp.where(hit, weight_high, 0.0).astype(BF16))
            low_of.append(jnp.where(hit, weight_low, 0.0).astype(BF16))
        for pair in range(n_tiles // 2):
            left = jnp.concatenate([rows_of[(2 * pair - 1) % n_tiles], rows_of[2 * pair], rows_of[2 * pair + 1]], axis=0)
            right_high = jnp.concatenate([high_of[2 * pair], high_of[2 * pair + 1]], axis=0)
            right_low = jnp.concatenate([low_of[2 * pair], low_of[2 * pair + 1]], axis=0)
            acc_ref[pair] += lax.dot_general(
                jnp.concatenate([left, left], axis=1),
                jnp.concatenate([right_high, right_low], axis=1),
                (((1,), (1,)), ((), ())),
                preferred_element_type=F32,
            )
        return carry

    lax.fori_loop(0, bonds // chunk, add_bonds, 0)
    same = lax.broadcasted_iota(jnp.int32, (pair_len, pair_len), 0) == lax.broadcasted_iota(jnp.int32, (pair_len, pair_len), 1)
    zero = jnp.zeros((tile_len, tile_len), BF16)
    n_pairs = n_tiles // 2
    for pair in range(n_pairs):
        inner = acc_ref[pair, tile_len:, :]
        middle = split(inner + inner.T + jnp.where(same, 1.0, 0.0))
        above = split(acc_ref[pair, :tile_len, :tile_len])
        below = split(acc_ref[(pair + 1) % n_pairs, :tile_len, :tile_len].T)
        for part in range(2):
            base = part * 2 * pair_len
            weight_ref[pair, base : base + tile_len, :] = jnp.concatenate([above[part], zero], axis=1)
            weight_ref[pair, base + tile_len : base + tile_len + pair_len, :] = middle[part]
            weight_ref[pair, base + tile_len + pair_len : base + 2 * pair_len, :] = jnp.concatenate([zero, below[part]], axis=1)


def green_kernel(
    n_tiles, tile_len, coupling, tile_cols_ref, where_ref, field_ref, weight_ref,
    out_ref, factor_ref, z_ref, a_ref, b_ref, c_ref, d_ref, low_ref,
):
    order = cycle_order(tile_cols_ref, n_tiles)
    slices, matrix_order = field_ref.shape
    n_pairs = n_tiles // 2
    pair_len = 2 * tile_len
    sign = 1.0 - 2.0 * where_ref[0].astype(F32)
    for p in range(n_tiles):
        spins_pm = (2 * field_ref[:, tile_ds(order[p], tile_len)] - 1).astype(F32)
        factor_ref[:, p * tile_len : (p + 1) * tile_len] = jnp.exp(sign * coupling * spins_pm)

    for p in range(n_tiles):
        row = factor_ref[slices - 1 : slices, p * tile_len : (p + 1) * tile_len]
        column = jnp.broadcast_to(row, (tile_len, tile_len)).T
        column = jnp.concatenate([column, column], axis=1)
        for pair in range(n_pairs):
            slots = [(2 * pair - 1) % n_tiles, 2 * pair, 2 * pair + 1, (2 * pair + 2) % n_tiles]
            cell = jnp.zeros((tile_len, pair_len), F32)
            if p in slots:
                at = slots.index(p) * tile_len
                high = weight_ref[pair, at : at + tile_len, :].astype(F32)
                low = weight_ref[pair, 2 * pair_len + at : 2 * pair_len + at + tile_len, :].astype(F32)
                cell = column * (high + low)
            z_ref[p * tile_len : (p + 1) * tile_len, pair * pair_len : (pair + 1) * pair_len] = cell

    def near(x, pair):
        tiles = [(2 * pair - 1) % n_tiles, 2 * pair, 2 * pair + 1, (2 * pair + 2) % n_tiles]
        return [x[:, t * tile_len : (t + 1) * tile_len] for t in tiles]

    block = 2 * tile_len

    def slice_step(step, carry):
        factor = factor_ref[pl.ds(slices - 2 - step, 1), :]
        for start in range(0, matrix_order, block):
            high, low = split(z_ref[start : start + block, :] * factor)
            for pair in range(n_pairs):
                left = jnp.concatenate(near(high, pair) + near(low, pair) + near(high, pair), axis=1)
                whole = weight_ref[pair]
                right = jnp.concatenate([whole[: 2 * pair_len], whole], axis=0)
                z_ref[start : start + block, pair * pair_len : (pair + 1) * pair_len] = dot(left, right)
        return carry

    lax.fori_loop(0, slices - 1, slice_step, 0)

    col_max = jnp.max(jnp.sum(z_ref[...], axis=0, keepdims=True), axis=1, keepdims=True)
    z_ref[...] = z_ref[...] * (0.5 / col_max)
    p_high, p_low = split(z_ref[...])
    a_ref[...] = p_high
    low_ref[...] = p_low
    b_ref[...] = dot(a_ref[...], a_ref[...]).astype(BF16)
    d_ref[...] = dot(b_ref[...], b_ref[...]).astype(BF16)
    c_ref[...] = (b_ref[...].astype(F32) - z_ref[...] - dot(b_ref[...], a_ref[...])).astype(BF16)
    start_y = -(c_ref[...].astype(F32) + d_ref[...].astype(F32) + dot(c_ref[...], d_ref[...]))
    b_ref[...] = start_y.astype(BF16)
    for start in range(0, matrix_order, block):
        rows = slice(start, start + block)
        guess = b_ref[rows, :]
        residual = guess.astype(F32) - z_ref[rows, :] + (dot(guess, a_ref[...]) + dot(guess, low_ref[...]))
        y = guess.astype(F32) - residual + dot(residual.astype(BF16), b_ref[...])
        for i in range(block // tile_len):
            p = start // tile_len + i
            for q in range(n_tiles):
                out_ref[tile_ds(order[p], tile_len), tile_ds(order[q], tile_len)] = y[
                    i * tile_len : (i + 1) * tile_len, q * tile_len : (q + 1) * tile_len
                ]


def gather_blocks(field, axis):
    size = lax.axis_size(axis)
    held, count = [field], 1
    while count < size:
        grown = list(held)
        for step in range(1, 4):
            by = step * count
            if by >= size:
                break
            pairs = [((i + by) % size, i) for i in range(size)]
            packed = held[0] if len(held) == 1 else jnp.concatenate(held, axis=0)
            moved = lax.ppermute(packed, axis, pairs)
            grown.append(moved)
        held = grown
        count = min(size, count * 4)
        held = [jnp.concatenate(held, axis=0)]
    return held[0]


def per_device(ising_field, bond_sites, hopping, tile_cols):
    slices_here, matrix_order = ising_field.shape
    n_tiles = tile_cols.shape[0]
    tile_len = matrix_order // n_tiles
    pair_len = 2 * tile_len
    n_pairs = n_tiles // 2
    col_width = matrix_order // lax.axis_size("rows")
    total_slices = slices_here * lax.axis_size("tm")
    coupling = 1.5 / math.sqrt(total_slices)
    smem = pl.BlockSpec(memory_space=pltpu.SMEM)
    vmem = pl.BlockSpec(memory_space=pltpu.VMEM)
    field = gather_blocks(ising_field, "tm")
    weights = pl.pallas_call(
        functools.partial(kinetic_kernel, n_tiles, tile_len, 0.5 / total_slices),
        out_shape=jax.ShapeDtypeStruct((n_pairs, 4 * pair_len, pair_len), BF16),
        in_specs=[smem, vmem, vmem],
        out_specs=vmem,
        scratch_shapes=[pltpu.VMEM((n_pairs, tile_len + pair_len, pair_len), F32)],
        cost_estimate=pl.CostEstimate(flops=4 * 10**9, bytes_accessed=4 * 10**6, transcendentals=0),
        name="kinetic",
    )(tile_cols, bond_sites.T, hopping[None, :])
    where = lax.axis_index("spin").astype(jnp.int32)[None]
    square = (matrix_order, matrix_order)
    y = pl.pallas_call(
        functools.partial(green_kernel, n_tiles, tile_len, coupling),
        out_shape=jax.ShapeDtypeStruct(square, F32),
        in_specs=[smem, smem, vmem, vmem],
        out_specs=vmem,
        scratch_shapes=[pltpu.VMEM((total_slices, matrix_order), F32), pltpu.VMEM(square, F32)] + [pltpu.VMEM(square, BF16)] * 5,
        cost_estimate=pl.CostEstimate(flops=4 * 10**10, bytes_accessed=6 * 10**6, transcendentals=0),
        name="green",
    )(tile_cols, where, field, weights)
    offset = lax.axis_index("rows") * col_width
    own_rows = lax.dynamic_slice_in_dim(y, offset, col_width, 0)
    size = lax.axis_size("spin")
    other_rows = lax.ppermute(own_rows, "spin", [(i, (i + 1) % size) for i in range(size)])
    own_cols = lax.dynamic_slice_in_dim(y, offset, col_width, 1)
    row_ids = jnp.arange(matrix_order, dtype=jnp.int32)[:, None]
    col_ids = offset + jnp.arange(col_width, dtype=jnp.int32)[None, :]
    eye_cols = (row_ids == col_ids).astype(F32)
    xcorr = (eye_cols - own_cols) * other_rows.T
    return xcorr[None, None]


def solution(mesh):
    placed = (P(("grp", "tm"), None), P(), P(), P())
    return jax.shard_map(
        per_device,
        mesh=mesh,
        in_specs=placed,
        out_specs=P("spin", ("grp", "tm"), None, "rows"),
        check_vma=False,
    )
```

```python
import functools
import math

import jax
import jax.numpy as jnp
from jax import lax
from jax.experimental import pallas as pl
from jax.experimental.pallas import tpu as pltpu
from jax.sharding import PartitionSpec as P

F32 = jnp.float32
BF16 = jnp.bfloat16


def dot(left, right):
    return jnp.dot(left, right, preferred_element_type=F32)


def split(x):
    high = x.astype(BF16)
    return high, (x - high.astype(F32)).astype(BF16)


def cycle_order(tile_cols_ref, n_tiles):
    order = [jnp.int32(0), tile_cols_ref[1, 0]]
    while len(order) < n_tiles:
        before, here = order[-2], order[-1]
        one, two = tile_cols_ref[1, here], tile_cols_ref[2, here]
        order.append(jnp.where(one == before, two, one))
    return order


def place_of(order, tile):
    place = jnp.int32(0)
    for p in range(1, len(order)):
        place = jnp.where(order[p] == tile, p, place)
    return place


def tile_ds(tile, tile_len):
    return pl.ds(pl.multiple_of(tile * tile_len, tile_len), tile_len)


def kinetic_kernel(n_tiles, tile_len, scale, tile_cols_ref, sites_ref, hopping_ref, weight_ref, acc_ref):
    order = cycle_order(tile_cols_ref, n_tiles)
    shift = tile_len.bit_length() - 1
    bonds = sites_ref.shape[1]
    pair_len = 2 * tile_len
    chunk = min(bonds, 512)

    def position(site):
        tile = site >> shift
        place = jnp.zeros_like(site)
        for p in range(1, n_tiles):
            place = jnp.where(tile == order[p], p, place)
        return place, place * tile_len + (site & (tile_len - 1))

    acc_ref[...] = jnp.zeros_like(acc_ref)

    def add_bonds(step, carry):
        lanes = pl.ds(pl.multiple_of(step * chunk, chunk), chunk)
        tile_a, site_a = position(sites_ref[0:1, lanes])
        tile_b, site_b = position(sites_ref[1:2, lanes])
        apart = jnp.abs(tile_a - tile_b)
        kept = (apart <= 1) | (apart == n_tiles - 1)
        weight = jnp.where(kept, hopping_ref[0:1, lanes] * scale, 0.0)
        weight_high = weight.astype(BF16).astype(F32)
        weight_low = weight - weight_high
        swap = ((tile_a >> 1) != (tile_b >> 1)) & ((tile_a & 1) == 0)
        first = jnp.where(swap, site_b, site_a)
        second = jnp.where(swap, site_a, site_b)
        row_ids = lax.broadcasted_iota(jnp.int32, (tile_len, chunk), 0)
        high_of, low_of, ones_of = [], [], []
        for p in range(n_tiles):
            ids = row_ids + p * tile_len
            hit = first == ids
            high_of.append(jnp.where(hit, weight_high, 0.0).astype(BF16))
            low_of.append(jnp.where(hit, weight_low, 0.0).astype(BF16))
            ones_of.append(jnp.where(second == ids, 1.0, 0.0).astype(BF16))
        for pair in range(n_tiles // 2):
            tiles = [(2 * pair - 1) % n_tiles, 2 * pair, 2 * pair + 1]
            left = jnp.concatenate([high_of[t] for t in tiles] + [low_of[t] for t in tiles], axis=0)
            right = jnp.concatenate([ones_of[2 * pair], ones_of[2 * pair + 1]], axis=0)
            both = lax.dot_general(left, right, (((1,), (1,)), ((), ())), preferred_element_type=F32)
            half = tile_len + pair_len
            acc_ref[pair] += both[:half] + both[half:]
        return carry

    lax.fori_loop(0, bonds // chunk, add_bonds, 0)
    same = lax.broadcasted_iota(jnp.int32, (pair_len, pair_len), 0) == lax.broadcasted_iota(jnp.int32, (pair_len, pair_len), 1)
    zero = jnp.zeros((tile_len, tile_len), BF16)
    n_pairs = n_tiles // 2
    for pair in range(n_pairs):
        inner = acc_ref[pair, tile_len:, :]
        high, low = split(inner + inner.T + jnp.where(same, 1.0, 0.0))
        weight_ref[pair, :pair_len, :] = high
        weight_ref[pair, pair_len : 2 * pair_len, :] = low
        above = acc_ref[pair, :tile_len, :tile_len]
        below = acc_ref[(pair + 1) % n_pairs, :tile_len, :tile_len].T
        for side, cell in enumerate((above, below)):
            high, low = split(cell)
            base = (2 + side) * pair_len
            weight_ref[pair, base : base + tile_len, :] = jnp.concatenate([high, low], axis=1)
            weight_ref[pair, base + tile_len : base + pair_len, :] = jnp.concatenate([high, zero], axis=1)


def chain(n_tiles, tile_len, factor_ref, weight_ref, z_ref):
    slices, matrix_order = factor_ref.shape
    n_pairs = n_tiles // 2
    pair_len = 2 * tile_len

    for p in range(n_tiles):
        row = factor_ref[slices - 1 : slices, p * tile_len : (p + 1) * tile_len]
        column = jnp.broadcast_to(row, (tile_len, tile_len)).T
        rows = slice(p * tile_len, (p + 1) * tile_len)
        z_ref[rows, :] = jnp.zeros((tile_len, matrix_order), F32)
        own = p // 2
        at = (p % 2) * tile_len
        whole = weight_ref[own, at : at + tile_len, :].astype(F32) + weight_ref[own, pair_len + at : pair_len + at + tile_len, :].astype(F32)
        z_ref[rows, own * pair_len : (own + 1) * pair_len] = jnp.concatenate([column, column], axis=1) * whole
        if p % 2:
            into, base, to = (own + 1) % n_pairs, 2 * pair_len, 0
        else:
            into, base, to = (own - 1) % n_pairs, 3 * pair_len, tile_len
        cell = weight_ref[into, base : base + tile_len, :].astype(F32)
        to = into * pair_len + to
        z_ref[rows, to : to + tile_len] = column * (cell[:, :tile_len] + cell[:, tile_len:])

    def tile(x, t):
        t = t % n_tiles
        return x[:, t * tile_len : (t + 1) * tile_len]

    def one_slice(index):
        factor = factor_ref[pl.ds(index, 1), :]
        for start in range(0, matrix_order, tile_len):
            rows = slice(start, start + tile_len)
            high, low = split(z_ref[rows, :] * factor)
            for pair in range(n_pairs):
                lanes = slice(pair * pair_len, (pair + 1) * pair_len)
                weight = weight_ref[pair]
                inner = dot(
                    jnp.concatenate([high[:, lanes], low[:, lanes], high[:, lanes]], axis=1),
                    jnp.concatenate([weight[:pair_len], weight[:pair_len], weight[pair_len : 2 * pair_len]], axis=0),
                )
                sides = []
                for side, t in enumerate((2 * pair - 1, 2 * pair + 2)):
                    base = (2 + side) * pair_len
                    part = dot(jnp.concatenate([tile(high, t), tile(low, t)], axis=1), weight[base : base + pair_len])
                    sides.append(part[:, :tile_len] + part[:, tile_len:])
                z_ref[rows, lanes] = inner + jnp.concatenate(sides, axis=1)

    steps = slices - 1
    together = 3 if steps % 3 == 0 else 1

    def some_slices(step, carry):
        for i in range(together):
            one_slice(slices - 2 - step * together - i)
        return carry

    lax.fori_loop(0, steps // together, some_slices, 0)


def corrected(guess, p_high_rows, p_low_rows, p_high_ref, p_low_ref, guess_ref):
    guess32 = guess.astype(F32)
    p_rows = p_high_rows.astype(F32) + p_low_rows.astype(F32)
    residual = (guess32 - p_rows) + (dot(guess, p_high_ref[...]) + dot(guess, p_low_ref[...]))
    return guess32 - residual + dot(residual.astype(BF16), guess_ref[...])


def tiles_of_rows(where_ref, n_tiles, own_tiles):
    first = where_ref[1] * own_tiles
    own = [first + i for i in range(own_tiles)]
    rest = [jnp.where(first <= i, i + own_tiles, i) for i in range(n_tiles - own_tiles)]
    return own, rest


def rows_at(ref, places, tile_len):
    return jnp.concatenate([ref[tile_ds(p, tile_len), :] for p in places], axis=0)


def green_kernel(
    n_tiles, tile_len, own_tiles, coupling, tile_cols_ref, where_ref, field_ref, weight_ref,
    rows_ref, guess_ref, p_high_ref, p_low_ref, factor_ref, z_ref, b_ref, c_ref, d_ref,
):
    order = cycle_order(tile_cols_ref, n_tiles)
    matrix_order = field_ref.shape[1]
    sign = 1.0 - 2.0 * where_ref[0].astype(F32)
    for p in range(n_tiles):
        spins_pm = (2 * field_ref[:, tile_ds(order[p], tile_len)] - 1).astype(F32)
        factor_ref[:, p * tile_len : (p + 1) * tile_len] = jnp.exp(sign * coupling * spins_pm)
    chain(n_tiles, tile_len, factor_ref, weight_ref, z_ref)

    block = 2 * tile_len
    blocks = [slice(start, start + block) for start in range(0, matrix_order, block)]
    col_max = jnp.max(jnp.sum(z_ref[...], axis=0, keepdims=True), axis=1, keepdims=True)
    shrink = 0.5 / col_max
    for rows in blocks:
        p_rows = z_ref[rows, :] * shrink
        p_high_ref[rows, :], p_low_ref[rows, :] = split(p_rows)
    for rows in blocks:
        b_ref[rows, :] = dot(p_high_ref[rows, :], p_high_ref[...]).astype(BF16)
    for rows in blocks:
        square = b_ref[rows, :]
        cube = dot(square, p_high_ref[...])
        c_ref[rows, :] = (square.astype(F32) - p_high_ref[rows, :].astype(F32) - p_low_ref[rows, :].astype(F32) - cube).astype(BF16)
        d_ref[rows, :] = dot(square, b_ref[...]).astype(BF16)
    for rows in blocks:
        part = c_ref[rows, :]
        guess_ref[rows, :] = (-(part.astype(F32) + d_ref[rows, :].astype(F32) + dot(part, d_ref[...]))).astype(BF16)

    own, _ = tiles_of_rows(where_ref, n_tiles, own_tiles)
    places = [place_of(order, t) for t in own]
    y = corrected(
        rows_at(guess_ref, places, tile_len), rows_at(p_high_ref, places, tile_len), rows_at(p_low_ref, places, tile_len),
        p_high_ref, p_low_ref, guess_ref,
    )
    for q in range(n_tiles):
        rows_ref[:, tile_ds(order[q], tile_len)] = y[:, q * tile_len : (q + 1) * tile_len]


def rest_kernel(n_tiles, tile_len, own_tiles, tile_cols_ref, where_ref, guess_ref, p_high_ref, p_low_ref, out_ref, y_ref):
    order = cycle_order(tile_cols_ref, n_tiles)
    own, rest = tiles_of_rows(where_ref, n_tiles, own_tiles)
    places = [place_of(order, t) for t in rest]
    y_ref[...] = corrected(
        rows_at(guess_ref, places, tile_len), rows_at(p_high_ref, places, tile_len), rows_at(p_low_ref, places, tile_len),
        p_high_ref, p_low_ref, guess_ref,
    )
    for i, t in enumerate(own):
        out_ref[:, i * tile_len : (i + 1) * tile_len] = y_ref[:, tile_ds(place_of(order, t), tile_len)]


def xcorr_kernel(n_tiles, tile_len, own_tiles, where_ref, rows_ref, rest_ref, other_ref, out_ref):
    own, rest = tiles_of_rows(where_ref, n_tiles, own_tiles)
    width = own_tiles * tile_len
    for i, t in enumerate(own):
        rows = slice(i * tile_len, (i + 1) * tile_len)
        for j, u in enumerate(own):
            cols = slice(j * tile_len, (j + 1) * tile_len)
            green = -rows_ref[rows, tile_ds(u, tile_len)]
            if i == j:
                ids = (tile_len, tile_len)
                green += jnp.where(lax.broadcasted_iota(jnp.int32, ids, 0) == lax.broadcasted_iota(jnp.int32, ids, 1), 1.0, 0.0)
            out_ref[tile_ds(t, tile_len), cols] = green * other_ref[cols, tile_ds(t, tile_len)].T
    for i, t in enumerate(rest):
        rows = slice(i * tile_len, (i + 1) * tile_len)
        for j in range(own_tiles):
            cols = slice(j * tile_len, (j + 1) * tile_len)
            out_ref[tile_ds(t, tile_len), cols] = -rest_ref[rows, cols] * other_ref[cols, tile_ds(t, tile_len)].T


def gather_blocks(field, axis):
    size = lax.axis_size(axis)
    held, count = [field], 1
    while count < size:
        grown = list(held)
        for step in range(1, 4):
            by = step * count
            if by >= size:
                break
            pairs = [((i + by) % size, i) for i in range(size)]
            packed = held[0] if len(held) == 1 else jnp.concatenate(held, axis=0)
            moved = lax.ppermute(packed, axis, pairs)
            grown.append(moved)
        held = grown
        count = min(size, count * 4)
        held = [jnp.concatenate(held, axis=0)]
    return held[0]


def per_device(ising_field, bond_sites, hopping, tile_cols):
    slices_here, matrix_order = ising_field.shape
    n_tiles = tile_cols.shape[0]
    tile_len = matrix_order // n_tiles
    pair_len = 2 * tile_len
    n_pairs = n_tiles // 2
    n_rows = lax.axis_size("rows")
    shared = 1
    while (n_tiles * shared) % n_rows:
        shared += 1
    own_tiles = n_tiles * shared // n_rows
    own_len = own_tiles * tile_len
    col_width = matrix_order // n_rows
    total_slices = slices_here * lax.axis_size("tm")
    coupling = 1.5 / math.sqrt(total_slices)
    smem = pl.BlockSpec(memory_space=pltpu.SMEM)
    vmem = pl.BlockSpec(memory_space=pltpu.VMEM)
    field = gather_blocks(ising_field, "tm")
    cols_of_tiles = tile_cols.T
    weights = pl.pallas_call(
        functools.partial(kinetic_kernel, n_tiles, tile_len, 0.5 / total_slices),
        out_shape=jax.ShapeDtypeStruct((n_pairs, 4 * pair_len, pair_len), BF16),
        in_specs=[smem, vmem, vmem],
        out_specs=vmem,
        scratch_shapes=[pltpu.VMEM((n_pairs, tile_len + pair_len, pair_len), F32)],
        compiler_params=pltpu.CompilerParams(vmem_limit_bytes=24 * 2**20),
        cost_estimate=pl.CostEstimate(flops=4 * 10**9, bytes_accessed=4 * 10**6, transcendentals=0),
        name="kinetic",
    )(cols_of_tiles, bond_sites.T, hopping[None, :])
    where = jnp.stack([lax.axis_index("spin"), lax.axis_index("rows") // shared]).astype(jnp.int32)
    square = (matrix_order, matrix_order)
    sizes = (n_tiles, tile_len, own_tiles)
    rows, guess, p_high, p_low = pl.pallas_call(
        functools.partial(green_kernel, *sizes, coupling),
        out_shape=[jax.ShapeDtypeStruct((own_len, matrix_order), F32)] + [jax.ShapeDtypeStruct(square, BF16)] * 3,
        in_specs=[smem, smem, vmem, vmem],
        out_specs=[vmem] * 4,
        scratch_shapes=[pltpu.VMEM((total_slices, matrix_order), F32), pltpu.VMEM(square, F32)] + [pltpu.VMEM(square, BF16)] * 3,
        compiler_params=pltpu.CompilerParams(vmem_limit_bytes=32 * 2**20),
        cost_estimate=pl.CostEstimate(flops=4 * 10**10, bytes_accessed=6 * 10**6, transcendentals=0),
        name="green",
    )(cols_of_tiles, where, field, weights)
    size = lax.axis_size("spin")
    other_rows = lax.ppermute(rows, "spin", [(i, (i + 1) % size) for i in range(size)])
    rest = pl.pallas_call(
        functools.partial(rest_kernel, *sizes),
        out_shape=jax.ShapeDtypeStruct((matrix_order - own_len, own_len), F32),
        in_specs=[smem, smem, vmem, vmem, vmem],
        out_specs=vmem,
        scratch_shapes=[pltpu.VMEM((matrix_order - own_len, matrix_order), F32)],
        compiler_params=pltpu.CompilerParams(vmem_limit_bytes=24 * 2**20),
        cost_estimate=pl.CostEstimate(flops=2 * 10**9, bytes_accessed=4 * 10**6, transcendentals=0),
        name="rest",
    )(cols_of_tiles, where, guess, p_high, p_low)
    xcorr = pl.pallas_call(
        functools.partial(xcorr_kernel, *sizes),
        out_shape=jax.ShapeDtypeStruct((matrix_order, own_len), F32),
        in_specs=[smem, vmem, vmem, vmem],
        out_specs=vmem,
        compiler_params=pltpu.CompilerParams(vmem_limit_bytes=16 * 2**20),
        name="xcorr",
    )(where, rows, rest, other_rows)
    if own_len != col_width:
        xcorr = lax.dynamic_slice_in_dim(xcorr, (lax.axis_index("rows") % shared) * col_width, col_width, 1)
    return xcorr[None, None]


def solution(mesh):
    placed = (P(("grp", "tm"), None), P(), P(), P())
    return jax.shard_map(
        per_device,
        mesh=mesh,
        in_specs=placed,
        out_specs=P("spin", ("grp", "tm"), None, "rows"),
        check_vma=False,
    )
```

```python
import functools
import math

import jax
import jax.numpy as jnp
from jax import lax
from jax.experimental import pallas as pl
from jax.experimental.pallas import tpu as pltpu
from jax.sharding import PartitionSpec as P

F32 = jnp.float32
BF16 = jnp.bfloat16
F8 = jnp.float8_e4m3fn


def dot(left, right):
    return jnp.dot(left, right, preferred_element_type=F32)


def split(x):
    high = x.astype(BF16)
    return high, (x - high.astype(F32)).astype(BF16)


def cycle_order(tile_cols_ref, n_tiles):
    order = [jnp.int32(0), tile_cols_ref[1, 0]]
    while len(order) < n_tiles:
        before, here = order[-2], order[-1]
        one, two = tile_cols_ref[1, here], tile_cols_ref[2, here]
        order.append(jnp.where(one == before, two, one))
    return order


def place_of(order, tile):
    place = jnp.int32(0)
    for p in range(1, len(order)):
        place = jnp.where(order[p] == tile, p, place)
    return place


def tile_ds(tile, tile_len):
    return pl.ds(pl.multiple_of(tile * tile_len, tile_len), tile_len)


def kinetic_kernel(
    n_tiles, tile_len, scale, tile_cols_hbm, sites_hbm, hopping_hbm, weight_ref, acc_ref, tile_cols_ref, sites_ref, hopping_ref, sems
):
    copies = [
        pltpu.make_async_copy(source, target, sems.at[i])
        for i, (source, target) in enumerate(((tile_cols_hbm, tile_cols_ref), (sites_hbm, sites_ref), (hopping_hbm, hopping_ref)))
    ]
    for copy in copies:
        copy.start()
    acc_ref[...] = jnp.zeros_like(acc_ref)
    for copy in copies:
        copy.wait()
    order = cycle_order(tile_cols_ref, n_tiles)
    shift = tile_len.bit_length() - 1
    bonds = sites_ref.shape[1]
    pair_len = 2 * tile_len
    chunk = min(bonds, 512)

    def position(site):
        tile = site >> shift
        place = jnp.zeros_like(site)
        for p in range(1, n_tiles):
            place = jnp.where(tile == order[p], p, place)
        return place, place * tile_len + (site & (tile_len - 1))

    def add_bonds(step):
        lanes = slice(step * chunk, (step + 1) * chunk)
        tile_a, site_a = position(sites_ref[0:1, lanes])
        tile_b, site_b = position(sites_ref[1:2, lanes])
        apart = jnp.abs(tile_a - tile_b)
        kept = (apart <= 1) | (apart == n_tiles - 1)
        weight = jnp.where(kept, hopping_ref[0:1, lanes] * scale, 0.0)
        weight_high = weight.astype(BF16).astype(F32)
        weight_low = weight - weight_high
        swap = ((tile_a >> 1) != (tile_b >> 1)) & ((tile_a & 1) == 0)
        first = jnp.where(swap, site_b, site_a)
        second = jnp.where(swap, site_a, site_b)
        row_ids = lax.broadcasted_iota(jnp.int32, (tile_len, chunk), 0)
        high_of, low_of, ones_of = [], [], []
        for p in range(n_tiles):
            ids = row_ids + p * tile_len
            hit = first == ids
            high_of.append(jnp.where(hit, weight_high, 0.0).astype(BF16))
            low_of.append(jnp.where(hit, weight_low, 0.0).astype(BF16))
            ones_of.append(jnp.where(second == ids, 1.0, 0.0).astype(BF16))
        for pair in range(n_tiles // 2):
            tiles = [(2 * pair - 1) % n_tiles, 2 * pair, 2 * pair + 1]
            left = jnp.concatenate([high_of[t] for t in tiles] + [low_of[t] for t in tiles], axis=0)
            right = jnp.concatenate([ones_of[2 * pair], ones_of[2 * pair + 1]], axis=0)
            both = lax.dot_general(left, right, (((1,), (1,)), ((), ())), preferred_element_type=F32)
            half = tile_len + pair_len
            acc_ref[pair] += both[:half] + both[half:]

    for step in range(bonds // chunk):
        add_bonds(step)
    same = lax.broadcasted_iota(jnp.int32, (pair_len, pair_len), 0) == lax.broadcasted_iota(jnp.int32, (pair_len, pair_len), 1)
    zero = jnp.zeros((tile_len, tile_len), BF16)
    n_pairs = n_tiles // 2
    for pair in range(n_pairs):
        inner = acc_ref[pair, tile_len:, :]
        high, low = split(inner + inner.T + jnp.where(same, 1.0, 0.0))
        weight_ref[pair, :pair_len, :] = high
        weight_ref[pair, pair_len : 2 * pair_len, :] = low
        above = acc_ref[pair, :tile_len, :tile_len]
        below = acc_ref[(pair + 1) % n_pairs, :tile_len, :tile_len].T
        for side, cell in enumerate((above, below)):
            high, low = split(cell)
            base = (2 + side) * pair_len
            weight_ref[pair, base : base + tile_len, :] = jnp.concatenate([high, low], axis=1)
            weight_ref[pair, base + tile_len : base + pair_len, :] = jnp.concatenate([high, zero], axis=1)


def chain(n_tiles, tile_len, factor_ref, weight_ref, z_ref):
    slices, matrix_order = factor_ref.shape
    n_pairs = n_tiles // 2
    pair_len = 2 * tile_len

    for p in range(n_tiles):
        row = factor_ref[slices - 1 : slices, p * tile_len : (p + 1) * tile_len]
        column = jnp.broadcast_to(row, (tile_len, tile_len)).T
        rows = slice(p * tile_len, (p + 1) * tile_len)
        z_ref[rows, :] = jnp.zeros((tile_len, matrix_order), F32)
        own = p // 2
        at = (p % 2) * tile_len
        whole = weight_ref[own, at : at + tile_len, :].astype(F32) + weight_ref[own, pair_len + at : pair_len + at + tile_len, :].astype(F32)
        z_ref[rows, own * pair_len : (own + 1) * pair_len] = jnp.concatenate([column, column], axis=1) * whole
        if p % 2:
            into, base, to = (own + 1) % n_pairs, 2 * pair_len, 0
        else:
            into, base, to = (own - 1) % n_pairs, 3 * pair_len, tile_len
        cell = weight_ref[into, base : base + tile_len, :].astype(F32)
        to = into * pair_len + to
        z_ref[rows, to : to + tile_len] = column * (cell[:, :tile_len] + cell[:, tile_len:])

    def tile(x, t):
        t = t % n_tiles
        return x[:, t * tile_len : (t + 1) * tile_len]

    def one_slice(index):
        factor = factor_ref[pl.ds(index, 1), :]
        for start in range(0, matrix_order, tile_len):
            rows = slice(start, start + tile_len)
            high, low = split(z_ref[rows, :] * factor)
            for pair in range(n_pairs):
                lanes = slice(pair * pair_len, (pair + 1) * pair_len)
                weight = weight_ref[pair]
                inner = dot(
                    jnp.concatenate([high[:, lanes], low[:, lanes], high[:, lanes]], axis=1),
                    jnp.concatenate([weight[:pair_len], weight[:pair_len], weight[pair_len : 2 * pair_len]], axis=0),
                )
                for side, t in enumerate((2 * pair - 1, 2 * pair + 2)):
                    base = (2 + side) * pair_len
                    part = dot(jnp.concatenate([tile(high, t), tile(low, t)], axis=1), weight[base : base + pair_len])
                    at = slice(side * tile_len, (side + 1) * tile_len)
                    to = (2 * pair + side) * tile_len
                    z_ref[rows, to : to + tile_len] = inner[:, at] + (part[:, :tile_len] + part[:, tile_len:])

    steps = slices - 1
    together = 3 if steps % 3 == 0 else 1

    def some_slices(step, carry):
        for i in range(together):
            one_slice(slices - 2 - step * together - i)
        return carry

    lax.fori_loop(0, steps // together, some_slices, 0)


def corrected(places, tile_len, p_high_ref, p_low_ref, guess_ref):
    def rows_of(ref):
        return jnp.concatenate([ref[tile_ds(p, tile_len), :] for p in places], axis=0)

    guess = rows_of(guess_ref)
    guess32 = guess.astype(F32)
    p_rows = rows_of(p_high_ref).astype(F32) + rows_of(p_low_ref).astype(F32)
    residual = (guess32 - p_rows) + (dot(guess, p_high_ref[...]) + dot(guess, p_low_ref[...]))
    return guess32 - residual + dot(residual.astype(BF16), guess_ref[...])


def tiles_of_rows(where_ref, n_tiles, own_tiles):
    first = where_ref[1] * own_tiles
    own = [first + i for i in range(own_tiles)]
    rest = [jnp.where(first <= i, i + own_tiles, i) for i in range(n_tiles - own_tiles)]
    return own, rest


def chain_kernel(n_tiles, tile_len, coupling, tile_cols_ref, where_ref, field_ref, weight_ref, z_ref, factor_ref):
    order = cycle_order(tile_cols_ref, n_tiles)
    sign = 1.0 - 2.0 * where_ref[0].astype(F32)
    for p in range(n_tiles):
        spins_pm = (2 * field_ref[:, tile_ds(order[p], tile_len)] - 1).astype(F32)
        factor_ref[:, p * tile_len : (p + 1) * tile_len] = jnp.exp(sign * coupling * spins_pm)
    chain(n_tiles, tile_len, factor_ref, weight_ref, z_ref)


def green_kernel(
    n_tiles, tile_len, own_tiles, tile_cols_ref, where_ref, z_ref,
    rows_ref, guess_ref, p_high_ref, p_low_ref, b_ref, c_ref, one8_ref, two8_ref, part8_ref, four8_ref,
):
    order = cycle_order(tile_cols_ref, n_tiles)
    matrix_order = z_ref.shape[1]
    block = 2 * tile_len
    blocks = [slice(start, start + block) for start in range(0, matrix_order, block)]
    col_max = jnp.max(jnp.sum(z_ref[...], axis=0, keepdims=True), axis=1, keepdims=True)
    shrink = 0.5 / col_max
    for rows in blocks:
        p_rows = z_ref[rows, :] * shrink
        p_high_ref[rows, :], p_low_ref[rows, :] = split(p_rows)
        one8_ref[rows, :] = (p_rows * 2.0**9).astype(F8)
    for rows in blocks:
        square = dot(p_high_ref[rows, :], p_high_ref[...])
        b_ref[rows, :] = square.astype(BF16)
        two8_ref[rows, :] = (square * 2.0**10).astype(F8)
    for rows in blocks:
        square = two8_ref[rows, :]
        cube = dot(square, one8_ref[...]) * 2.0**-19
        part = b_ref[rows, :].astype(F32) - p_high_ref[rows, :].astype(F32) - cube
        fourth = dot(square, two8_ref[...]) * 2.0**-20
        c_ref[rows, :] = part + fourth
        part8_ref[rows, :] = (part * 2.0**8).astype(F8)
        four8_ref[rows, :] = (fourth * 2.0**12).astype(F8)
    for rows in blocks:
        guess_ref[rows, :] = (-(c_ref[rows, :] + dot(part8_ref[rows, :], four8_ref[...]) * 2.0**-20)).astype(BF16)

    own, _ = tiles_of_rows(where_ref, n_tiles, own_tiles)
    y = corrected([place_of(order, t) for t in own], tile_len, p_high_ref, p_low_ref, guess_ref)
    for q in range(n_tiles):
        rows_ref[:, tile_ds(order[q], tile_len)] = y[:, q * tile_len : (q + 1) * tile_len]


def rest_kernel(n_tiles, tile_len, own_tiles, tile_cols_ref, where_ref, guess_ref, p_high_ref, p_low_ref, out_ref, y_ref):
    order = cycle_order(tile_cols_ref, n_tiles)
    own, rest = tiles_of_rows(where_ref, n_tiles, own_tiles)
    y_ref[...] = corrected([place_of(order, t) for t in rest], tile_len, p_high_ref, p_low_ref, guess_ref)
    for i, t in enumerate(own):
        out_ref[:, i * tile_len : (i + 1) * tile_len] = y_ref[:, tile_ds(place_of(order, t), tile_len)]


def xcorr_kernel(n_tiles, tile_len, own_tiles, where_ref, rows_ref, rest_ref, other_ref, out_ref):
    own, rest = tiles_of_rows(where_ref, n_tiles, own_tiles)
    width = own_tiles * tile_len
    for i, t in enumerate(own):
        rows = slice(i * tile_len, (i + 1) * tile_len)
        for j, u in enumerate(own):
            cols = slice(j * tile_len, (j + 1) * tile_len)
            green = -rows_ref[rows, tile_ds(u, tile_len)]
            if i == j:
                ids = (tile_len, tile_len)
                green += jnp.where(lax.broadcasted_iota(jnp.int32, ids, 0) == lax.broadcasted_iota(jnp.int32, ids, 1), 1.0, 0.0)
            out_ref[tile_ds(t, tile_len), cols] = green * other_ref[cols, tile_ds(t, tile_len)].T
    for i, t in enumerate(rest):
        rows = slice(i * tile_len, (i + 1) * tile_len)
        for j in range(own_tiles):
            cols = slice(j * tile_len, (j + 1) * tile_len)
            out_ref[tile_ds(t, tile_len), cols] = -rest_ref[rows, cols] * other_ref[cols, tile_ds(t, tile_len)].T


def gather_blocks(field, axis):
    size = lax.axis_size(axis)
    held, count = [field], 1
    while count < size:
        grown = list(held)
        for step in range(1, 4):
            by = step * count
            if by >= size:
                break
            pairs = [((i + by) % size, i) for i in range(size)]
            packed = held[0] if len(held) == 1 else jnp.concatenate(held, axis=0)
            moved = lax.ppermute(packed, axis, pairs)
            grown.append(moved)
        held = grown
        count = min(size, count * 4)
        held = [jnp.concatenate(held, axis=0)]
    return held[0]


def per_device(ising_field, bond_sites, hopping, tile_cols):
    slices_here, matrix_order = ising_field.shape
    n_tiles = tile_cols.shape[0]
    tile_len = matrix_order // n_tiles
    pair_len = 2 * tile_len
    n_pairs = n_tiles // 2
    n_rows = lax.axis_size("rows")
    shared = 1
    while (n_tiles * shared) % n_rows:
        shared += 1
    own_tiles = n_tiles * shared // n_rows
    own_len = own_tiles * tile_len
    col_width = matrix_order // n_rows
    total_slices = slices_here * lax.axis_size("tm")
    coupling = 1.5 / math.sqrt(total_slices)
    smem = pl.BlockSpec(memory_space=pltpu.SMEM)
    vmem = pl.BlockSpec(memory_space=pltpu.VMEM)
    field = gather_blocks(ising_field, "tm")
    cols_of_tiles = tile_cols.T
    weights = pl.pallas_call(
        functools.partial(kinetic_kernel, n_tiles, tile_len, 0.5 / total_slices),
        out_shape=jax.ShapeDtypeStruct((n_pairs, 4 * pair_len, pair_len), BF16),
        in_specs=[pl.BlockSpec(memory_space=pltpu.HBM)] * 3,
        out_specs=vmem,
        scratch_shapes=[
            pltpu.VMEM((n_pairs, tile_len + pair_len, pair_len), F32),
            pltpu.SMEM(cols_of_tiles.shape, jnp.int32),
            pltpu.VMEM((2, hopping.shape[0]), jnp.int32),
            pltpu.VMEM((1, hopping.shape[0]), F32),
            pltpu.SemaphoreType.DMA((3,)),
        ],
        compiler_params=pltpu.CompilerParams(vmem_limit_bytes=24 * 2**20),
        cost_estimate=pl.CostEstimate(flops=4 * 10**9, bytes_accessed=4 * 10**6, transcendentals=0),
        name="kinetic",
    )(*[pltpu.with_memory_space_constraint(x, pltpu.HBM) for x in (cols_of_tiles, bond_sites.T, hopping[None, :])])
    where = jnp.stack([lax.axis_index("spin"), lax.axis_index("rows") // shared]).astype(jnp.int32)
    square = (matrix_order, matrix_order)
    sizes = (n_tiles, tile_len, own_tiles)
    product = pl.pallas_call(
        functools.partial(chain_kernel, n_tiles, tile_len, coupling),
        out_shape=jax.ShapeDtypeStruct(square, F32),
        in_specs=[smem, smem, vmem, vmem],
        out_specs=vmem,
        scratch_shapes=[pltpu.VMEM((total_slices, matrix_order), F32)],
        compiler_params=pltpu.CompilerParams(vmem_limit_bytes=24 * 2**20),
        cost_estimate=pl.CostEstimate(flops=3 * 10**10, bytes_accessed=4 * 10**6, transcendentals=0),
        name="chain",
    )(cols_of_tiles, where, field, weights)
    rows, guess, p_high, p_low = pl.pallas_call(
        functools.partial(green_kernel, *sizes),
        out_shape=[jax.ShapeDtypeStruct((own_len, matrix_order), F32)] + [jax.ShapeDtypeStruct(square, BF16)] * 3,
        in_specs=[smem, smem, vmem],
        out_specs=[vmem] * 4,
        scratch_shapes=[pltpu.VMEM(square, BF16), pltpu.VMEM(square, F32)]
        + [pltpu.VMEM(square, F8)] * 4,
        compiler_params=pltpu.CompilerParams(vmem_limit_bytes=32 * 2**20),
        cost_estimate=pl.CostEstimate(flops=5 * 10**9, bytes_accessed=6 * 10**6, transcendentals=0),
        name="green",
    )(cols_of_tiles, where, product)
    size = lax.axis_size("spin")
    other_rows = lax.ppermute(rows, "spin", [(i, (i + 1) % size) for i in range(size)])
    rest = pl.pallas_call(
        functools.partial(rest_kernel, *sizes),
        out_shape=jax.ShapeDtypeStruct((matrix_order - own_len, own_len), F32),
        in_specs=[smem, smem, vmem, vmem, vmem],
        out_specs=vmem,
        scratch_shapes=[pltpu.VMEM((matrix_order - own_len, matrix_order), F32)],
        compiler_params=pltpu.CompilerParams(vmem_limit_bytes=24 * 2**20),
        cost_estimate=pl.CostEstimate(flops=2 * 10**9, bytes_accessed=4 * 10**6, transcendentals=0),
        name="rest",
    )(cols_of_tiles, where, guess, p_high, p_low)
    xcorr = pl.pallas_call(
        functools.partial(xcorr_kernel, *sizes),
        out_shape=jax.ShapeDtypeStruct((matrix_order, own_len), F32),
        in_specs=[smem, vmem, vmem, vmem],
        out_specs=vmem,
        compiler_params=pltpu.CompilerParams(vmem_limit_bytes=16 * 2**20),
        name="xcorr",
    )(where, rows, rest, other_rows)
    if own_len != col_width:
        xcorr = lax.dynamic_slice_in_dim(xcorr, (lax.axis_index("rows") % shared) * col_width, col_width, 1)
    return xcorr[None, None]


def solution(mesh):
    placed = (P(("grp", "tm"), None), P(), P(), P())
    return jax.shard_map(
        per_device,
        mesh=mesh,
        in_specs=placed,
        out_specs=P("spin", ("grp", "tm"), None, "rows"),
        check_vma=False,
    )
```

```python
import functools
import math

import jax
import jax.numpy as jnp
from jax import lax
from jax.experimental import pallas as pl
from jax.experimental.pallas import tpu as pltpu
from jax.sharding import PartitionSpec as P

F32 = jnp.float32
BF16 = jnp.bfloat16
F8 = jnp.float8_e4m3fn


def dot(left, right):
    return jnp.dot(left, right, preferred_element_type=F32)


def split(x):
    high = x.astype(BF16)
    return high, (x - high.astype(F32)).astype(BF16)


def cycle_order(tile_cols_ref, n_tiles):
    order = [jnp.int32(0), tile_cols_ref[1, 0]]
    while len(order) < n_tiles:
        before, here = order[-2], order[-1]
        one, two = tile_cols_ref[1, here], tile_cols_ref[2, here]
        order.append(jnp.where(one == before, two, one))
    return order


def place_of(order, tile):
    place = jnp.int32(0)
    for p in range(1, len(order)):
        place = jnp.where(order[p] == tile, p, place)
    return place


def tile_ds(tile, tile_len):
    return pl.ds(pl.multiple_of(tile * tile_len, tile_len), tile_len)


def kinetic_kernel(
    n_tiles, tile_len, scale, tile_cols_hbm, sites_hbm, hopping_hbm, weight_ref, acc_ref, tile_cols_ref, sites_ref, hopping_ref, sems
):
    copies = [
        pltpu.make_async_copy(source, target, sems.at[i])
        for i, (source, target) in enumerate(((tile_cols_hbm, tile_cols_ref), (sites_hbm, sites_ref), (hopping_hbm, hopping_ref)))
    ]
    for copy in copies:
        copy.start()
    acc_ref[...] = jnp.zeros_like(acc_ref)
    for copy in copies:
        copy.wait()
    order = cycle_order(tile_cols_ref, n_tiles)
    shift = tile_len.bit_length() - 1
    bonds = sites_ref.shape[1]
    pair_len = 2 * tile_len
    chunk = min(bonds, 512)

    def position(site):
        tile = site >> shift
        place = jnp.zeros_like(site)
        for p in range(1, n_tiles):
            place = jnp.where(tile == order[p], p, place)
        return place, place * tile_len + (site & (tile_len - 1))

    def add_bonds(step):
        lanes = slice(step * chunk, (step + 1) * chunk)
        tile_a, site_a = position(sites_ref[0:1, lanes])
        tile_b, site_b = position(sites_ref[1:2, lanes])
        apart = jnp.abs(tile_a - tile_b)
        kept = (apart <= 1) | (apart == n_tiles - 1)
        weight = jnp.where(kept, hopping_ref[0:1, lanes] * scale, 0.0)
        weight_high = weight.astype(BF16).astype(F32)
        weight_low = weight - weight_high
        together = (tile_a >> 1) == (tile_b >> 1)
        swap = (tile_a != tile_b) & (together == ((tile_a & 1) == 1))
        first = jnp.where(swap, site_b, site_a)
        second = jnp.where(swap, site_a, site_b)
        slot = jnp.where(together, first, second - (second & (tile_len - 1)) + tile_len + (first & (tile_len - 1)))
        row_ids = lax.broadcasted_iota(jnp.int32, (tile_len, chunk), 0)
        high_of, low_of, ones_of = [], [], []
        for p in range(n_tiles):
            ids = row_ids + p * tile_len
            hit = slot == ids
            high_of.append(jnp.where(hit, weight_high, 0.0).astype(BF16))
            low_of.append(jnp.where(hit, weight_low, 0.0).astype(BF16))
            ones_of.append(jnp.where(second == ids, 1.0, 0.0).astype(BF16))
        for pair in range(n_tiles // 2):
            tiles = [2 * pair, 2 * pair + 1]
            left = jnp.concatenate([high_of[t] for t in tiles] + [low_of[t] for t in tiles], axis=0)
            right = jnp.concatenate([ones_of[2 * pair], ones_of[2 * pair + 1]], axis=0)
            both = lax.dot_general(left, right, (((1,), (1,)), ((), ())), preferred_element_type=F32)
            acc_ref[pair] += both[:pair_len] + both[pair_len:]

    for step in range(bonds // chunk):
        add_bonds(step)
    same = lax.broadcasted_iota(jnp.int32, (pair_len, pair_len), 0) == lax.broadcasted_iota(jnp.int32, (pair_len, pair_len), 1)
    zero = jnp.zeros((tile_len, tile_len), BF16)
    n_pairs = n_tiles // 2
    for pair in range(n_pairs):
        lower = acc_ref[pair, tile_len:, :]
        lower = jnp.concatenate([jnp.zeros((tile_len, tile_len), F32), lower[:, tile_len:]], axis=1)
        inner = jnp.concatenate([acc_ref[pair, :tile_len, :], lower], axis=0)
        high, low = split(inner + inner.T + jnp.where(same, 1.0, 0.0))
        weight_ref[pair, :pair_len, :] = high
        weight_ref[pair, pair_len : 2 * pair_len, :] = low
        above = acc_ref[pair, tile_len:, :tile_len]
        below = acc_ref[(pair + 1) % n_pairs, tile_len:, :tile_len].T
        for side, cell in enumerate((above, below)):
            high, low = split(cell)
            base = (2 + side) * pair_len
            weight_ref[pair, base : base + tile_len, :] = jnp.concatenate([high, low], axis=1)
            weight_ref[pair, base + tile_len : base + pair_len, :] = jnp.concatenate([high, zero], axis=1)


def chain(n_tiles, tile_len, factor_ref, weight_ref, z_ref):
    slices, matrix_order = factor_ref.shape
    n_pairs = n_tiles // 2
    pair_len = 2 * tile_len

    for p in range(n_tiles):
        row = factor_ref[slices - 1 : slices, p * tile_len : (p + 1) * tile_len]
        column = jnp.broadcast_to(row, (tile_len, tile_len)).T
        rows = slice(p * tile_len, (p + 1) * tile_len)
        z_ref[rows, :] = jnp.zeros((tile_len, matrix_order), F32)
        own = p // 2
        at = (p % 2) * tile_len
        whole = weight_ref[own, at : at + tile_len, :].astype(F32) + weight_ref[own, pair_len + at : pair_len + at + tile_len, :].astype(F32)
        z_ref[rows, own * pair_len : (own + 1) * pair_len] = jnp.concatenate([column, column], axis=1) * whole
        if p % 2:
            into, base, to = (own + 1) % n_pairs, 2 * pair_len, 0
        else:
            into, base, to = (own - 1) % n_pairs, 3 * pair_len, tile_len
        cell = weight_ref[into, base : base + tile_len, :].astype(F32)
        to = into * pair_len + to
        z_ref[rows, to : to + tile_len] = column * (cell[:, :tile_len] + cell[:, tile_len:])

    def tile(x, t):
        t = t % n_tiles
        return x[:, t * tile_len : (t + 1) * tile_len]

    def one_slice(index, reach):
        factor = factor_ref[pl.ds(index, 1), :]
        for p in range(n_tiles):
            rows = slice(p * tile_len, (p + 1) * tile_len)
            high, low = split(z_ref[rows, :] * factor)

            def live(t):
                apart = (t - p) % n_tiles
                return min(apart, n_tiles - apart) <= reach

            for pair in range(n_pairs):
                lanes = slice(pair * pair_len, (pair + 1) * pair_len)
                weight = weight_ref[pair]
                inner = None
                if live(2 * pair) or live(2 * pair + 1):
                    inner = dot(
                        jnp.concatenate([high[:, lanes], low[:, lanes], high[:, lanes]], axis=1),
                        jnp.concatenate([weight[:pair_len], weight[:pair_len], weight[pair_len : 2 * pair_len]], axis=0),
                    )
                for side, t in enumerate((2 * pair - 1, 2 * pair + 2)):
                    parts = [] if inner is None else [inner[:, side * tile_len : (side + 1) * tile_len]]
                    if live(t):
                        base = (2 + side) * pair_len
                        part = dot(jnp.concatenate([tile(high, t), tile(low, t)], axis=1), weight[base : base + pair_len])
                        parts.append(part[:, :tile_len] + part[:, tile_len:])
                    to = (2 * pair + side) * tile_len
                    z_ref[rows, to : to + tile_len] = sum(parts) if parts else jnp.zeros((tile_len, tile_len), F32)

    steps = slices - 1
    peeled = steps if steps <= 16 else n_tiles // 2
    for step in range(peeled):
        one_slice(steps - 1 - step, step + 1)
    if peeled < steps:
        lax.fori_loop(peeled, steps, lambda step, carry: (one_slice(steps - 1 - step, n_tiles), carry)[1], 0)


def corrected(places, tile_len, p_high_ref, p_low_ref, guess_ref):
    def rows_of(ref):
        return jnp.concatenate([ref[tile_ds(p, tile_len), :] for p in places], axis=0)

    guess = rows_of(guess_ref)
    guess32 = guess.astype(F32)
    p_rows = rows_of(p_high_ref).astype(F32) + rows_of(p_low_ref).astype(F32)
    residual = (guess32 - p_rows) + (dot(guess, p_high_ref[...]) + dot(guess, p_low_ref[...]))
    return guess32 - residual + dot(residual.astype(BF16), guess_ref[...])


def tiles_of_rows(where_ref, n_tiles, own_tiles):
    first = where_ref[1] * own_tiles
    own = [first + i for i in range(own_tiles)]
    rest = [jnp.where(first <= i, i + own_tiles, i) for i in range(n_tiles - own_tiles)]
    return own, rest


def chain_kernel(n_tiles, tile_len, coupling, tile_cols_ref, where_ref, field_ref, weight_ref, z_ref, factor_ref):
    order = cycle_order(tile_cols_ref, n_tiles)
    sign = 1.0 - 2.0 * where_ref[0].astype(F32)
    for p in range(n_tiles):
        spins_pm = (2 * field_ref[:, tile_ds(order[p], tile_len)] - 1).astype(F32)
        factor_ref[:, p * tile_len : (p + 1) * tile_len] = jnp.exp(sign * coupling * spins_pm)
    chain(n_tiles, tile_len, factor_ref, weight_ref, z_ref)


def green_kernel(
    n_tiles, tile_len, own_tiles, tile_cols_ref, where_ref, z_ref,
    rows_ref, guess_ref, p_high_ref, p_low_ref, b_ref, c_ref, one8_ref, two8_ref, part8_ref, four8_ref,
):
    order = cycle_order(tile_cols_ref, n_tiles)
    matrix_order = z_ref.shape[1]
    block = 2 * tile_len
    blocks = [slice(start, start + block) for start in range(0, matrix_order, block)]
    col_max = jnp.max(jnp.sum(z_ref[...], axis=0, keepdims=True), axis=1, keepdims=True)
    shrink = 0.5 / col_max
    for rows in blocks:
        p_rows = z_ref[rows, :] * shrink
        p_high_ref[rows, :], p_low_ref[rows, :] = split(p_rows)
        one8_ref[rows, :] = (p_rows * 2.0**9).astype(F8)
    for rows in blocks:
        square = dot(p_high_ref[rows, :], p_high_ref[...])
        b_ref[rows, :] = square.astype(BF16)
        two8_ref[rows, :] = (square * 2.0**10).astype(F8)
    for rows in blocks:
        square = two8_ref[rows, :]
        cube = dot(square, one8_ref[...]) * 2.0**-19
        part = b_ref[rows, :].astype(F32) - p_high_ref[rows, :].astype(F32) - cube
        fourth = dot(square, two8_ref[...]) * 2.0**-20
        c_ref[rows, :] = part + fourth
        part8_ref[rows, :] = (part * 2.0**8).astype(F8)
        four8_ref[rows, :] = (fourth * 2.0**12).astype(F8)
    for rows in blocks:
        guess_ref[rows, :] = (-(c_ref[rows, :] + dot(part8_ref[rows, :], four8_ref[...]) * 2.0**-20)).astype(BF16)

    own, _ = tiles_of_rows(where_ref, n_tiles, own_tiles)
    y = corrected([place_of(order, t) for t in own], tile_len, p_high_ref, p_low_ref, guess_ref)
    for q in range(n_tiles):
        rows_ref[:, tile_ds(order[q], tile_len)] = y[:, q * tile_len : (q + 1) * tile_len]


def rest_kernel(n_tiles, tile_len, own_tiles, tile_cols_ref, where_ref, guess_ref, p_high_ref, p_low_ref, out_ref, y_ref):
    order = cycle_order(tile_cols_ref, n_tiles)
    own, rest = tiles_of_rows(where_ref, n_tiles, own_tiles)
    y_ref[...] = corrected([place_of(order, t) for t in rest], tile_len, p_high_ref, p_low_ref, guess_ref)
    for i, t in enumerate(own):
        out_ref[:, i * tile_len : (i + 1) * tile_len] = y_ref[:, tile_ds(place_of(order, t), tile_len)]


def xcorr_kernel(n_tiles, tile_len, own_tiles, where_ref, rows_ref, rest_ref, other_ref, out_ref):
    own, rest = tiles_of_rows(where_ref, n_tiles, own_tiles)
    width = own_tiles * tile_len
    for i, t in enumerate(own):
        rows = slice(i * tile_len, (i + 1) * tile_len)
        for j, u in enumerate(own):
            cols = slice(j * tile_len, (j + 1) * tile_len)
            green = -rows_ref[rows, tile_ds(u, tile_len)]
            if i == j:
                ids = (tile_len, tile_len)
                green += jnp.where(lax.broadcasted_iota(jnp.int32, ids, 0) == lax.broadcasted_iota(jnp.int32, ids, 1), 1.0, 0.0)
            out_ref[tile_ds(t, tile_len), cols] = green * other_ref[cols, tile_ds(t, tile_len)].T
    for i, t in enumerate(rest):
        rows = slice(i * tile_len, (i + 1) * tile_len)
        for j in range(own_tiles):
            cols = slice(j * tile_len, (j + 1) * tile_len)
            out_ref[tile_ds(t, tile_len), cols] = -rest_ref[rows, cols] * other_ref[cols, tile_ds(t, tile_len)].T


def gather_blocks(field, axis):
    size = lax.axis_size(axis)
    held, count = [field], 1
    while count < size:
        grown = list(held)
        for step in range(1, 4):
            by = step * count
            if by >= size:
                break
            pairs = [((i + by) % size, i) for i in range(size)]
            packed = held[0] if len(held) == 1 else jnp.concatenate(held, axis=0)
            moved = lax.ppermute(packed, axis, pairs)
            grown.append(moved)
        held = grown
        count = min(size, count * 4)
        held = [jnp.concatenate(held, axis=0)]
    return held[0]


def per_device(ising_field, bond_sites, hopping, tile_cols):
    slices_here, matrix_order = ising_field.shape
    n_tiles = tile_cols.shape[0]
    tile_len = matrix_order // n_tiles
    pair_len = 2 * tile_len
    n_pairs = n_tiles // 2
    n_rows = lax.axis_size("rows")
    shared = 1
    while (n_tiles * shared) % n_rows:
        shared += 1
    own_tiles = n_tiles * shared // n_rows
    own_len = own_tiles * tile_len
    col_width = matrix_order // n_rows
    total_slices = slices_here * lax.axis_size("tm")
    coupling = 1.5 / math.sqrt(total_slices)
    smem = pl.BlockSpec(memory_space=pltpu.SMEM)
    vmem = pl.BlockSpec(memory_space=pltpu.VMEM)
    field = gather_blocks(ising_field, "tm")
    cols_of_tiles = tile_cols.T
    weights = pl.pallas_call(
        functools.partial(kinetic_kernel, n_tiles, tile_len, 0.5 / total_slices),
        out_shape=jax.ShapeDtypeStruct((n_pairs, 4 * pair_len, pair_len), BF16),
        in_specs=[pl.BlockSpec(memory_space=pltpu.HBM)] * 3,
        out_specs=vmem,
        scratch_shapes=[
            pltpu.VMEM((n_pairs, pair_len, pair_len), F32),
            pltpu.SMEM(cols_of_tiles.shape, jnp.int32),
            pltpu.VMEM((2, hopping.shape[0]), jnp.int32),
            pltpu.VMEM((1, hopping.shape[0]), F32),
            pltpu.SemaphoreType.DMA((3,)),
        ],
        compiler_params=pltpu.CompilerParams(vmem_limit_bytes=24 * 2**20),
        cost_estimate=pl.CostEstimate(flops=4 * 10**9, bytes_accessed=4 * 10**6, transcendentals=0),
        name="kinetic",
    )(*[pltpu.with_memory_space_constraint(x, pltpu.HBM) for x in (cols_of_tiles, bond_sites.T, hopping[None, :])])
    where = jnp.stack([lax.axis_index("spin"), lax.axis_index("rows") // shared]).astype(jnp.int32)
    square = (matrix_order, matrix_order)
    sizes = (n_tiles, tile_len, own_tiles)
    product = pl.pallas_call(
        functools.partial(chain_kernel, n_tiles, tile_len, coupling),
        out_shape=jax.ShapeDtypeStruct(square, F32),
        in_specs=[smem, smem, vmem, vmem],
        out_specs=vmem,
        scratch_shapes=[pltpu.VMEM((total_slices, matrix_order), F32)],
        compiler_params=pltpu.CompilerParams(vmem_limit_bytes=24 * 2**20),
        cost_estimate=pl.CostEstimate(flops=3 * 10**10, bytes_accessed=4 * 10**6, transcendentals=0),
        name="chain",
    )(cols_of_tiles, where, field, weights)
    rows, guess, p_high, p_low = pl.pallas_call(
        functools.partial(green_kernel, *sizes),
        out_shape=[jax.ShapeDtypeStruct((own_len, matrix_order), F32)] + [jax.ShapeDtypeStruct(square, BF16)] * 3,
        in_specs=[smem, smem, vmem],
        out_specs=[vmem] * 4,
        scratch_shapes=[pltpu.VMEM(square, BF16), pltpu.VMEM(square, F32)]
        + [pltpu.VMEM(square, F8)] * 4,
        compiler_params=pltpu.CompilerParams(vmem_limit_bytes=32 * 2**20),
        cost_estimate=pl.CostEstimate(flops=5 * 10**9, bytes_accessed=6 * 10**6, transcendentals=0),
        name="green",
    )(cols_of_tiles, where, product)
    size = lax.axis_size("spin")
    other_rows = lax.ppermute(rows, "spin", [(i, (i + 1) % size) for i in range(size)])
    rest = pl.pallas_call(
        functools.partial(rest_kernel, *sizes),
        out_shape=jax.ShapeDtypeStruct((matrix_order - own_len, own_len), F32),
        in_specs=[smem, smem, vmem, vmem, vmem],
        out_specs=vmem,
        scratch_shapes=[pltpu.VMEM((matrix_order - own_len, matrix_order), F32)],
        compiler_params=pltpu.CompilerParams(vmem_limit_bytes=24 * 2**20),
        cost_estimate=pl.CostEstimate(flops=2 * 10**9, bytes_accessed=4 * 10**6, transcendentals=0),
        name="rest",
    )(cols_of_tiles, where, guess, p_high, p_low)
    xcorr = pl.pallas_call(
        functools.partial(xcorr_kernel, *sizes),
        out_shape=jax.ShapeDtypeStruct((matrix_order, own_len), F32),
        in_specs=[smem, vmem, vmem, vmem],
        out_specs=vmem,
        compiler_params=pltpu.CompilerParams(vmem_limit_bytes=16 * 2**20),
        name="xcorr",
    )(where, rows, rest, other_rows)
    if own_len != col_width:
        xcorr = lax.dynamic_slice_in_dim(xcorr, (lax.axis_index("rows") % shared) * col_width, col_width, 1)
    return xcorr[None, None]


def solution(mesh):
    placed = (P(("grp", "tm"), None), P(), P(), P())
    return jax.shard_map(
        per_device,
        mesh=mesh,
        in_specs=placed,
        out_specs=P("spin", ("grp", "tm"), None, "rows"),
        check_vma=False,
    )
```

```python
import functools
import math

import jax
import jax.numpy as jnp
from jax import lax
from jax.experimental import pallas as pl
from jax.experimental.pallas import tpu as pltpu
from jax.sharding import PartitionSpec as P

F32 = jnp.float32
BF16 = jnp.bfloat16
F8 = jnp.float8_e4m3fn


def dot(left, right):
    return jnp.dot(left, right, preferred_element_type=F32)


def split(x):
    high = x.astype(BF16)
    return high, (x - high.astype(F32)).astype(BF16)


def cycle_order(tile_cols_ref, n_tiles):
    order = [jnp.int32(0), tile_cols_ref[1, 0]]
    while len(order) < n_tiles:
        before, here = order[-2], order[-1]
        one, two = tile_cols_ref[1, here], tile_cols_ref[2, here]
        order.append(jnp.where(one == before, two, one))
    return order


def place_of(order, tile):
    place = jnp.int32(0)
    for p in range(1, len(order)):
        place = jnp.where(order[p] == tile, p, place)
    return place


def tile_ds(tile, tile_len):
    return pl.ds(pl.multiple_of(tile * tile_len, tile_len), tile_len)


def kinetic_kernel(
    n_tiles, tile_len, scale, tile_cols_hbm, sites_hbm, hopping_hbm, weight_ref, acc_ref, tile_cols_ref, sites_ref, hopping_ref, sems
):
    copies = [
        pltpu.make_async_copy(source, target, sems.at[i])
        for i, (source, target) in enumerate(((tile_cols_hbm, tile_cols_ref), (sites_hbm, sites_ref), (hopping_hbm, hopping_ref)))
    ]
    for copy in copies:
        copy.start()
    acc_ref[...] = jnp.zeros_like(acc_ref)
    for copy in copies:
        copy.wait()
    order = cycle_order(tile_cols_ref, n_tiles)
    shift = tile_len.bit_length() - 1
    bonds = sites_ref.shape[1]
    pair_len = 2 * tile_len
    chunk = min(bonds, 512)

    def position(site):
        tile = site >> shift
        place = jnp.zeros_like(site)
        for p in range(1, n_tiles):
            place = jnp.where(tile == order[p], p, place)
        return place, place * tile_len + (site & (tile_len - 1))

    def add_bonds(step):
        lanes = slice(step * chunk, (step + 1) * chunk)
        tile_a, site_a = position(sites_ref[0:1, lanes])
        tile_b, site_b = position(sites_ref[1:2, lanes])
        apart = jnp.abs(tile_a - tile_b)
        kept = (apart <= 1) | (apart == n_tiles - 1)
        weight = jnp.where(kept, hopping_ref[0:1, lanes] * scale, 0.0)
        weight_high = weight.astype(BF16).astype(F32)
        weight_low = weight - weight_high
        together = (tile_a >> 1) == (tile_b >> 1)
        swap = (tile_a != tile_b) & (together == ((tile_a & 1) == 1))
        first = jnp.where(swap, site_b, site_a)
        second = jnp.where(swap, site_a, site_b)
        slot = jnp.where(together, first, second - (second & (tile_len - 1)) + tile_len + (first & (tile_len - 1)))
        row_ids = lax.broadcasted_iota(jnp.int32, (tile_len, chunk), 0)
        high_of, low_of, ones_of = [], [], []
        for p in range(n_tiles):
            ids = row_ids + p * tile_len
            hit = slot == ids
            high_of.append(jnp.where(hit, weight_high, 0.0).astype(BF16))
            low_of.append(jnp.where(hit, weight_low, 0.0).astype(BF16))
            ones_of.append(jnp.where(second == ids, 1.0, 0.0).astype(BF16))
        for pair in range(n_tiles // 2):
            tiles = [2 * pair, 2 * pair + 1]
            left = jnp.concatenate([high_of[t] for t in tiles] + [low_of[t] for t in tiles], axis=0)
            right = jnp.concatenate([ones_of[2 * pair], ones_of[2 * pair + 1]], axis=0)
            both = lax.dot_general(left, right, (((1,), (1,)), ((), ())), preferred_element_type=F32)
            acc_ref[pair] += both[:pair_len] + both[pair_len:]

    for step in range(bonds // chunk):
        add_bonds(step)
    same = lax.broadcasted_iota(jnp.int32, (pair_len, pair_len), 0) == lax.broadcasted_iota(jnp.int32, (pair_len, pair_len), 1)
    zero = jnp.zeros((tile_len, tile_len), BF16)
    n_pairs = n_tiles // 2
    for pair in range(n_pairs):
        lower = acc_ref[pair, tile_len:, :]
        lower = jnp.concatenate([jnp.zeros((tile_len, tile_len), F32), lower[:, tile_len:]], axis=1)
        inner = jnp.concatenate([acc_ref[pair, :tile_len, :], lower], axis=0)
        high, low = split(inner + inner.T + jnp.where(same, 1.0, 0.0))
        weight_ref[pair, :pair_len, :] = high
        weight_ref[pair, pair_len : 2 * pair_len, :] = low
        above = acc_ref[pair, tile_len:, :tile_len]
        below = acc_ref[(pair + 1) % n_pairs, tile_len:, :tile_len].T
        for side, cell in enumerate((above, below)):
            high, low = split(cell)
            base = (2 + side) * pair_len
            weight_ref[pair, base : base + tile_len, :] = jnp.concatenate([high, low], axis=1)
            weight_ref[pair, base + tile_len : base + pair_len, :] = jnp.concatenate([high, zero], axis=1)


def chain(n_tiles, tile_len, parity, factor_ref, weight_ref, targets):
    slices, matrix_order = factor_ref.shape
    n_pairs = n_tiles // 2
    pair_len = 2 * tile_len

    def first_rows(p):
        row = factor_ref[slices - 1 : slices, p * tile_len : (p + 1) * tile_len]
        column = jnp.broadcast_to(row, (tile_len, tile_len)).T
        own = p // 2
        at = (p % 2) * tile_len
        whole = weight_ref[own, at : at + tile_len, :].astype(F32) + weight_ref[own, pair_len + at : pair_len + at + tile_len, :].astype(F32)
        if p % 2:
            into, base, next_tile = (own + 1) % n_pairs, 2 * pair_len, (p + 1) % n_tiles
        else:
            into, base, next_tile = (own - 1) % n_pairs, 3 * pair_len, (p - 1) % n_tiles
        cell = weight_ref[into, base : base + tile_len, :].astype(F32)
        cells = [jnp.zeros((tile_len, tile_len), F32)] * n_tiles
        cells[2 * own] = column * whole[:, :tile_len]
        cells[2 * own + 1] = column * whole[:, tile_len:]
        cells[next_tile] = column * (cell[:, :tile_len] + cell[:, tile_len:])
        return jnp.concatenate(cells, axis=1)

    started = targets[0][1] is not None
    for z_ref, _, rows, tiles in [] if started else targets:
        z_ref[rows, :] = first_rows(tiles[0]) if len(tiles) == 1 else jnp.where(parity == 0, first_rows(tiles[0]), first_rows(tiles[1]))

    def tile(x, t):
        t = t % n_tiles
        return x[:, t * tile_len : (t + 1) * tile_len]

    def one_slice(index, reach, afresh=False):
        factor = factor_ref[pl.ds(index, 1), :]
        for z_ref, source_ref, rows, tiles in targets:
            high, low = split((source_ref if afresh else z_ref)[rows, :] * factor)

            def live(t):
                return any(min((t - p) % n_tiles, (p - t) % n_tiles) <= reach for p in tiles)

            for pair in range(n_pairs):
                lanes = slice(pair * pair_len, (pair + 1) * pair_len)
                weight = weight_ref[pair]
                inner = None
                if live(2 * pair) or live(2 * pair + 1):
                    inner = dot(
                        jnp.concatenate([high[:, lanes], low[:, lanes], high[:, lanes]], axis=1),
                        jnp.concatenate([weight[:pair_len], weight[:pair_len], weight[pair_len : 2 * pair_len]], axis=0),
                    )
                for side, t in enumerate((2 * pair - 1, 2 * pair + 2)):
                    parts = [] if inner is None else [inner[:, side * tile_len : (side + 1) * tile_len]]
                    if live(t):
                        base = (2 + side) * pair_len
                        part = dot(jnp.concatenate([tile(high, t), tile(low, t)], axis=1), weight[base : base + pair_len])
                        parts.append(part[:, :tile_len] + part[:, tile_len:])
                    to = (2 * pair + side) * tile_len
                    z_ref[rows, to : to + tile_len] = sum(parts) if parts else jnp.zeros((tile_len, tile_len), F32)

    steps = slices if started else slices - 1
    peeled = steps if steps <= 16 else n_tiles // 2
    for step in range(peeled):
        one_slice(steps - 1 - step, n_tiles if started else step + 1, started and step == 0)
    if peeled < steps:
        lax.fori_loop(peeled, steps, lambda step, carry: (one_slice(steps - 1 - step, n_tiles), carry)[1], 0)


def corrected(places, tile_len, p_high_ref, p_low_ref, guess_ref):
    def rows_of(ref):
        return jnp.concatenate([ref[tile_ds(p, tile_len), :] for p in places], axis=0)

    guess = rows_of(guess_ref)
    guess32 = guess.astype(F32)
    p_rows = rows_of(p_high_ref).astype(F32) + rows_of(p_low_ref).astype(F32)
    residual = (guess32 - p_rows) + (dot(guess, p_high_ref[...]) + dot(guess, p_low_ref[...]))
    return guess32 - residual + dot(residual.astype(BF16), guess_ref[...])


def tiles_of_rows(where_ref, n_tiles, own_tiles):
    first = where_ref[1] * own_tiles
    own = [first + i for i in range(own_tiles)]
    rest = [jnp.where(first <= i, i + own_tiles, i) for i in range(n_tiles - own_tiles)]
    return own, rest


def chain_kernel(n_tiles, tile_len, coupling, tiles_of, tile_cols_ref, where_ref, field_ref, weight_ref, *refs):
    *z_refs, factor_ref = refs
    parts = len(tiles_of)
    sources, z_refs = (z_refs[:-parts] or [None] * parts), z_refs[-parts:]
    order = cycle_order(tile_cols_ref, n_tiles)
    sign = 1.0 - 2.0 * where_ref[0].astype(F32)
    for p in range(n_tiles):
        spins_pm = (2 * field_ref[:, tile_ds(order[p], tile_len)] - 1).astype(F32)
        factor_ref[:, p * tile_len : (p + 1) * tile_len] = jnp.exp(sign * coupling * spins_pm)
    targets = []
    for z_ref, source_ref, tiles_in in zip(z_refs, sources, tiles_of):
        targets += [(z_ref, source_ref, slice(i * tile_len, (i + 1) * tile_len), tiles) for i, tiles in enumerate(tiles_in)]
    chain(n_tiles, tile_len, where_ref[2], factor_ref, weight_ref, targets)


def green_kernel(
    n_tiles, tile_len, own_tiles, tile_cols_ref, where_ref, mine_ref, theirs_ref, common_ref, last_ref,
    rows_ref, guess_ref, p_high_ref, p_low_ref, b_ref, c_ref, one8_ref, two8_ref, part8_ref, four8_ref,
):
    order = cycle_order(tile_cols_ref, n_tiles)
    matrix_order = mine_ref.shape[1]
    block = 2 * tile_len
    blocks = [slice(start, start + block) for start in range(0, matrix_order, block)]
    even = where_ref[2] == 0
    first, second = mine_ref[...], theirs_ref[...]
    pieces = [jnp.where(even, first, second), jnp.where(even, second, first)]
    for z_ref in (common_ref, last_ref):
        pieces += [z_ref[start : start + tile_len, :] for start in range(0, z_ref.shape[0], tile_len)]
    col_sum = sum(jnp.sum(piece, axis=0, keepdims=True) for piece in pieces)
    shrink = 0.5 / jnp.max(col_sum, axis=1, keepdims=True)
    for p, piece in enumerate(pieces):
        rows = slice(p * tile_len, (p + 1) * tile_len)
        p_rows = piece * shrink
        p_high_ref[rows, :], p_low_ref[rows, :] = split(p_rows)
        one8_ref[rows, :] = (p_rows * 2.0**9).astype(F8)
    for rows in blocks:
        square = dot(p_high_ref[rows, :], p_high_ref[...])
        b_ref[rows, :] = square.astype(BF16)
        two8_ref[rows, :] = (square * 2.0**10).astype(F8)
    for rows in blocks:
        square = two8_ref[rows, :]
        cube = dot(square, one8_ref[...]) * 2.0**-19
        part = b_ref[rows, :].astype(F32) - p_high_ref[rows, :].astype(F32) - cube
        fourth = dot(square, two8_ref[...]) * 2.0**-20
        c_ref[rows, :] = part + fourth
        part8_ref[rows, :] = (part * 2.0**8).astype(F8)
        four8_ref[rows, :] = (fourth * 2.0**12).astype(F8)
    for rows in blocks:
        guess_ref[rows, :] = (-(c_ref[rows, :] + dot(part8_ref[rows, :], four8_ref[...]) * 2.0**-20)).astype(BF16)

    own, _ = tiles_of_rows(where_ref, n_tiles, own_tiles)
    y = corrected([place_of(order, t) for t in own], tile_len, p_high_ref, p_low_ref, guess_ref)
    for q in range(n_tiles):
        rows_ref[:, tile_ds(order[q], tile_len)] = y[:, q * tile_len : (q + 1) * tile_len]


def rest_kernel(n_tiles, tile_len, own_tiles, tile_cols_ref, where_ref, guess_ref, p_high_ref, p_low_ref, out_ref, y_ref):
    order = cycle_order(tile_cols_ref, n_tiles)
    own, rest = tiles_of_rows(where_ref, n_tiles, own_tiles)
    y_ref[...] = corrected([place_of(order, t) for t in rest], tile_len, p_high_ref, p_low_ref, guess_ref)
    for i, t in enumerate(own):
        out_ref[:, i * tile_len : (i + 1) * tile_len] = y_ref[:, tile_ds(place_of(order, t), tile_len)]


def xcorr_kernel(n_tiles, tile_len, own_tiles, where_ref, rows_ref, rest_ref, other_ref, out_ref, block_ref, sems):
    own, rest = tiles_of_rows(where_ref, n_tiles, own_tiles)
    ids = (tile_len, tile_len)
    one = jnp.where(lax.broadcasted_iota(jnp.int32, ids, 0) == lax.broadcasted_iota(jnp.int32, ids, 1), 1.0, 0.0)
    copies = []
    for i, t in enumerate(own + rest):
        for j in range(own_tiles):
            cols = slice(j * tile_len, (j + 1) * tile_len)
            if i < own_tiles:
                green = -rows_ref[i * tile_len : (i + 1) * tile_len, tile_ds(own[j], tile_len)]
                if i == j:
                    green += one
            else:
                green = -rest_ref[(i - own_tiles) * tile_len : (i - own_tiles + 1) * tile_len, cols]
            block_ref[i, :, cols] = green * other_ref[cols, tile_ds(t, tile_len)].T
        copies.append(pltpu.make_async_copy(block_ref.at[i], out_ref.at[tile_ds(t, tile_len), :], sems.at[i]))
        copies[-1].start()
    for copy in copies:
        copy.wait()


def from_ahead(x, axis, by):
    size = lax.axis_size(axis)
    return lax.ppermute(x, axis, [((i + by) % size, i) for i in range(size)])


def gather_blocks(field, axis):
    size = lax.axis_size(axis)
    behind = from_ahead(field, axis, -1)
    held, by = jnp.concatenate([behind, field], axis=0), 2
    while by < size:
        held = jnp.concatenate([held, from_ahead(held, axis, by)], axis=0)
        by *= 2
    return behind, held[field.shape[0] :]


def per_device(ising_field, bond_sites, hopping, tile_cols):
    slices_here, matrix_order = ising_field.shape
    n_tiles = tile_cols.shape[0]
    tile_len = matrix_order // n_tiles
    pair_len = 2 * tile_len
    n_pairs = n_tiles // 2
    n_rows = lax.axis_size("rows")
    shared = 1
    while (n_tiles * shared) % n_rows:
        shared += 1
    own_tiles = n_tiles * shared // n_rows
    own_len = own_tiles * tile_len
    col_width = matrix_order // n_rows
    total_slices = slices_here * lax.axis_size("tm")
    coupling = 1.5 / math.sqrt(total_slices)
    smem = pl.BlockSpec(memory_space=pltpu.SMEM)
    vmem = pl.BlockSpec(memory_space=pltpu.VMEM)
    behind, ahead = gather_blocks(ising_field, "tm")
    cols_of_tiles = tile_cols.T
    weights = pl.pallas_call(
        functools.partial(kinetic_kernel, n_tiles, tile_len, 0.5 / total_slices),
        out_shape=jax.ShapeDtypeStruct((n_pairs, 4 * pair_len, pair_len), BF16),
        in_specs=[pl.BlockSpec(memory_space=pltpu.HBM)] * 3,
        out_specs=vmem,
        scratch_shapes=[
            pltpu.VMEM((n_pairs, pair_len, pair_len), F32),
            pltpu.SMEM(cols_of_tiles.shape, jnp.int32),
            pltpu.VMEM((2, hopping.shape[0]), jnp.int32),
            pltpu.VMEM((1, hopping.shape[0]), F32),
            pltpu.SemaphoreType.DMA((3,)),
        ],
        compiler_params=pltpu.CompilerParams(vmem_limit_bytes=24 * 2**20),
        cost_estimate=pl.CostEstimate(flops=4 * 10**9, bytes_accessed=4 * 10**6, transcendentals=0),
        name="kinetic",
    )(*[pltpu.with_memory_space_constraint(x, pltpu.HBM) for x in (cols_of_tiles, bond_sites.T, hopping[None, :])])
    where = jnp.stack([lax.axis_index("spin"), lax.axis_index("rows") // shared, lax.axis_index("rows") % 2]).astype(jnp.int32)
    square = (matrix_order, matrix_order)
    sizes = (n_tiles, tile_len, own_tiles)

    def chain_part(field, sources, *tiles_of):
        lengths = [len(tiles) * tile_len for tiles in tiles_of]
        return pl.pallas_call(
            functools.partial(chain_kernel, n_tiles, tile_len, coupling, tiles_of),
            out_shape=[jax.ShapeDtypeStruct((length, matrix_order), F32) for length in lengths],
            in_specs=[smem, smem] + [vmem] * (2 + len(sources)),
            out_specs=[vmem] * len(lengths),
            scratch_shapes=[pltpu.VMEM((field.shape[0], matrix_order), F32)],
            compiler_params=pltpu.CompilerParams(vmem_limit_bytes=24 * 2**20),
            cost_estimate=pl.CostEstimate(flops=25 * 10**5 * sum(lengths) * field.shape[0], bytes_accessed=4 * 10**6, transcendentals=0),
            name="chain",
        )(cols_of_tiles, where, field, weights, *sources)

    half = n_tiles // 2
    shared_tile, common_tiles, last_tiles = [(0, 1)], [(p,) for p in range(2, half)], [(p,) for p in range(half, n_tiles)]
    mine, common, last = chain_part(behind, [], shared_tile, common_tiles, last_tiles)
    mine, common = chain_part(ahead, [mine, common], shared_tile, common_tiles)
    theirs = lax.ppermute(mine, "rows", [(i, i ^ 1) for i in range(n_rows)])
    (last,) = chain_part(ahead, [last], last_tiles)
    rows, guess, p_high, p_low = pl.pallas_call(
        functools.partial(green_kernel, *sizes),
        out_shape=[jax.ShapeDtypeStruct((own_len, matrix_order), F32)] + [jax.ShapeDtypeStruct(square, BF16)] * 3,
        in_specs=[smem, smem] + [vmem] * 4,
        out_specs=[vmem] * 4,
        scratch_shapes=[pltpu.VMEM(square, BF16), pltpu.VMEM(square, F32)]
        + [pltpu.VMEM(square, F8)] * 4,
        compiler_params=pltpu.CompilerParams(vmem_limit_bytes=32 * 2**20),
        cost_estimate=pl.CostEstimate(flops=5 * 10**9, bytes_accessed=6 * 10**6, transcendentals=0),
        name="green",
    )(cols_of_tiles, where, mine, theirs, common, last)
    size = lax.axis_size("spin")
    other_rows = lax.ppermute(rows, "spin", [(i, (i + 1) % size) for i in range(size)])
    rest = pl.pallas_call(
        functools.partial(rest_kernel, *sizes),
        out_shape=jax.ShapeDtypeStruct((matrix_order - own_len, own_len), F32),
        in_specs=[smem, smem, vmem, vmem, vmem],
        out_specs=vmem,
        scratch_shapes=[pltpu.VMEM((matrix_order - own_len, matrix_order), F32)],
        compiler_params=pltpu.CompilerParams(vmem_limit_bytes=24 * 2**20),
        cost_estimate=pl.CostEstimate(flops=2 * 10**9, bytes_accessed=4 * 10**6, transcendentals=0),
        name="rest",
    )(cols_of_tiles, where, guess, p_high, p_low)
    xcorr = pl.pallas_call(
        functools.partial(xcorr_kernel, *sizes),
        out_shape=jax.ShapeDtypeStruct((matrix_order, own_len), F32),
        in_specs=[smem, vmem, vmem, vmem],
        out_specs=pl.BlockSpec(memory_space=pltpu.HBM),
        scratch_shapes=[pltpu.VMEM((n_tiles, tile_len, own_len), F32), pltpu.SemaphoreType.DMA((n_tiles,))],
        compiler_params=pltpu.CompilerParams(vmem_limit_bytes=16 * 2**20),
        name="xcorr",
    )(where, rows, rest, other_rows)
    if own_len != col_width:
        xcorr = lax.dynamic_slice_in_dim(xcorr, (lax.axis_index("rows") % shared) * col_width, col_width, 1)
    return xcorr[None, None]


def solution(mesh):
    placed = (P(("grp", "tm"), None), P(), P(), P())
    return jax.shard_map(
        per_device,
        mesh=mesh,
        in_specs=placed,
        out_specs=P("spin", ("grp", "tm"), None, "rows"),
        check_vma=False,
    )
```

```python
import functools
import math

import jax
import jax.numpy as jnp
from jax import lax
from jax.experimental import pallas as pl
from jax.experimental.pallas import tpu as pltpu
from jax.sharding import PartitionSpec as P

F32 = jnp.float32
BF16 = jnp.bfloat16
F8 = jnp.float8_e4m3fn


def dot(left, right):
    return jnp.dot(left, right, preferred_element_type=F32)


def dot_by(left, right, width):
    return jnp.concatenate([dot(left, right[:, at : at + width]) for at in range(0, right.shape[1], width)], axis=1)


def split(x):
    high = x.astype(BF16)
    return high, (x - high.astype(F32)).astype(BF16)


def cycle_order(tile_cols_ref, n_tiles):
    order = [jnp.int32(0), tile_cols_ref[1, 0]]
    while len(order) < n_tiles:
        before, here = order[-2], order[-1]
        one, two = tile_cols_ref[1, here], tile_cols_ref[2, here]
        order.append(jnp.where(one == before, two, one))
    return order


def place_of(order, tile):
    place = jnp.int32(0)
    for p in range(1, len(order)):
        place = jnp.where(order[p] == tile, p, place)
    return place


def tile_ds(tile, tile_len):
    return pl.ds(pl.multiple_of(tile * tile_len, tile_len), tile_len)


def kinetic_kernel(
    n_tiles, tile_len, scale, tile_cols_hbm, sites_hbm, hopping_hbm, weight_ref, acc_ref, tile_cols_ref, sites_ref, hopping_ref, sems
):
    copies = [
        pltpu.make_async_copy(source, target, sems.at[i])
        for i, (source, target) in enumerate(((tile_cols_hbm, tile_cols_ref), (sites_hbm, sites_ref), (hopping_hbm, hopping_ref)))
    ]
    for copy in copies:
        copy.start()
    acc_ref[...] = jnp.zeros_like(acc_ref)
    for copy in copies:
        copy.wait()
    order = cycle_order(tile_cols_ref, n_tiles)
    shift = tile_len.bit_length() - 1
    bonds = sites_ref.shape[1]
    pair_len = 2 * tile_len
    chunk = min(bonds, 512)

    def position(site):
        tile = site >> shift
        place = jnp.zeros_like(site)
        for p in range(1, n_tiles):
            place = jnp.where(tile == order[p], p, place)
        return place, place * tile_len + (site & (tile_len - 1))

    def add_bonds(step):
        lanes = slice(step * chunk, (step + 1) * chunk)
        tile_a, site_a = position(sites_ref[0:1, lanes])
        tile_b, site_b = position(sites_ref[1:2, lanes])
        apart = jnp.abs(tile_a - tile_b)
        kept = (apart <= 1) | (apart == n_tiles - 1)
        weight = jnp.where(kept, hopping_ref[0:1, lanes] * scale, 0.0)
        weight_high = weight.astype(BF16).astype(F32)
        weight_low = weight - weight_high
        together = (tile_a >> 1) == (tile_b >> 1)
        swap = (tile_a != tile_b) & (together == ((tile_a & 1) == 1))
        first = jnp.where(swap, site_b, site_a)
        second = jnp.where(swap, site_a, site_b)
        slot = jnp.where(together, first, second - (second & (tile_len - 1)) + tile_len + (first & (tile_len - 1)))
        row_ids = lax.broadcasted_iota(jnp.int32, (tile_len, chunk), 0)
        high_of, low_of, ones_of = [], [], []
        for p in range(n_tiles):
            ids = row_ids + p * tile_len
            hit = slot == ids
            high_of.append(jnp.where(hit, weight_high, 0.0).astype(BF16))
            low_of.append(jnp.where(hit, weight_low, 0.0).astype(BF16))
            ones_of.append(jnp.where(second == ids, 1.0, 0.0).astype(BF16))
        for pair in range(n_tiles // 2):
            tiles = [2 * pair, 2 * pair + 1]
            left = jnp.concatenate([high_of[t] for t in tiles] + [low_of[t] for t in tiles], axis=0)
            right = jnp.concatenate([ones_of[2 * pair], ones_of[2 * pair + 1]], axis=0)
            both = lax.dot_general(left, right, (((1,), (1,)), ((), ())), preferred_element_type=F32)
            acc_ref[pair] += both[:pair_len] + both[pair_len:]

    for step in range(bonds // chunk):
        add_bonds(step)
    same = lax.broadcasted_iota(jnp.int32, (pair_len, pair_len), 0) == lax.broadcasted_iota(jnp.int32, (pair_len, pair_len), 1)
    zero = jnp.zeros((tile_len, tile_len), BF16)
    n_pairs = n_tiles // 2
    for pair in range(n_pairs):
        lower = acc_ref[pair, tile_len:, :]
        lower = jnp.concatenate([jnp.zeros((tile_len, tile_len), F32), lower[:, tile_len:]], axis=1)
        inner = jnp.concatenate([acc_ref[pair, :tile_len, :], lower], axis=0)
        high, low = split(inner + inner.T + jnp.where(same, 1.0, 0.0))
        weight_ref[pair, :pair_len, :] = high
        weight_ref[pair, pair_len : 2 * pair_len, :] = low
        above = acc_ref[pair, tile_len:, :tile_len]
        below = acc_ref[(pair + 1) % n_pairs, tile_len:, :tile_len].T
        for side, cell in enumerate((above, below)):
            high, low = split(cell)
            base = (2 + side) * pair_len
            weight_ref[pair, base : base + tile_len, :] = jnp.concatenate([high, low], axis=1)
            weight_ref[pair, base + tile_len : base + pair_len, :] = jnp.concatenate([high, zero], axis=1)


def chain(n_tiles, tile_len, parity, factor_ref, weight_ref, targets):
    slices, matrix_order = factor_ref.shape
    n_pairs = n_tiles // 2
    pair_len = 2 * tile_len

    def first_rows(p):
        row = factor_ref[slices - 1 : slices, p * tile_len : (p + 1) * tile_len]
        column = jnp.broadcast_to(row, (tile_len, tile_len)).T
        own = p // 2
        at = (p % 2) * tile_len
        whole = weight_ref[own, at : at + tile_len, :].astype(F32) + weight_ref[own, pair_len + at : pair_len + at + tile_len, :].astype(F32)
        if p % 2:
            into, base, next_tile = (own + 1) % n_pairs, 2 * pair_len, (p + 1) % n_tiles
        else:
            into, base, next_tile = (own - 1) % n_pairs, 3 * pair_len, (p - 1) % n_tiles
        cell = weight_ref[into, base : base + tile_len, :].astype(F32)
        cells = [jnp.zeros((tile_len, tile_len), F32)] * n_tiles
        cells[2 * own] = column * whole[:, :tile_len]
        cells[2 * own + 1] = column * whole[:, tile_len:]
        cells[next_tile] = column * (cell[:, :tile_len] + cell[:, tile_len:])
        return jnp.concatenate(cells, axis=1)

    started = targets[0][1] is not None
    for z_ref, _, rows, tiles in [] if started else targets:
        z_ref[rows, :] = first_rows(tiles[0]) if len(tiles) == 1 else jnp.where(parity == 0, first_rows(tiles[0]), first_rows(tiles[1]))

    def tile(x, t):
        t = t % n_tiles
        return x[:, t * tile_len : (t + 1) * tile_len]

    def one_slice(index, reach, afresh=False):
        factor = factor_ref[pl.ds(index, 1), :]
        for z_ref, source_ref, rows, tiles in targets:
            high, low = split((source_ref if afresh else z_ref)[rows, :] * factor)

            def live(t):
                return any(min((t - p) % n_tiles, (p - t) % n_tiles) <= reach for p in tiles)

            for pair in range(n_pairs):
                lanes = slice(pair * pair_len, (pair + 1) * pair_len)
                weight = weight_ref[pair]
                inner = None
                if live(2 * pair) or live(2 * pair + 1):
                    inner = dot(
                        jnp.concatenate([high[:, lanes], low[:, lanes], high[:, lanes]], axis=1),
                        jnp.concatenate([weight[:pair_len], weight[:pair_len], weight[pair_len : 2 * pair_len]], axis=0),
                    )
                for side, t in enumerate((2 * pair - 1, 2 * pair + 2)):
                    parts = [] if inner is None else [inner[:, side * tile_len : (side + 1) * tile_len]]
                    if live(t):
                        base = (2 + side) * pair_len
                        part = dot(jnp.concatenate([tile(high, t), tile(low, t)], axis=1), weight[base : base + pair_len])
                        parts.append(part[:, :tile_len] + part[:, tile_len:])
                    to = (2 * pair + side) * tile_len
                    z_ref[rows, to : to + tile_len] = sum(parts) if parts else jnp.zeros((tile_len, tile_len), F32)

    steps = slices if started else slices - 1
    peeled = steps if steps <= 16 else n_tiles // 2
    for step in range(peeled):
        one_slice(steps - 1 - step, n_tiles if started else step + 1, started and step == 0)
    if peeled < steps:
        lax.fori_loop(peeled, steps, lambda step, carry: (one_slice(steps - 1 - step, n_tiles), carry)[1], 0)


def corrected(places, tile_len, excess_ref, p_high_ref, p_low_ref, guess_ref):
    def rows_of(ref):
        return jnp.concatenate([ref[tile_ds(p, tile_len), :] for p in places], axis=0)

    guess = rows_of(guess_ref)
    guess8 = (guess.astype(F32) * 2.0**8).astype(F8)
    small = dot_by(guess8, p_low_ref[...], 2 * tile_len) * 2.0**-25
    residual = rows_of(excess_ref) + dot_by(guess, p_high_ref[...], 2 * tile_len) + small
    return (guess.astype(F32) - residual) + dot_by(residual.astype(BF16), guess_ref[...], 2 * tile_len)


def tiles_of_rows(where_ref, n_tiles, own_tiles):
    first = where_ref[1] * own_tiles
    own = [first + i for i in range(own_tiles)]
    rest = [jnp.where(first <= i, i + own_tiles, i) for i in range(n_tiles - own_tiles)]
    return own, rest


def chain_kernel(n_tiles, tile_len, coupling, tiles_of, tile_cols_ref, where_ref, field_ref, weight_ref, *refs):
    *z_refs, factor_ref = refs
    parts = len(tiles_of)
    sources, z_refs = (z_refs[:-parts] or [None] * parts), z_refs[-parts:]
    order = cycle_order(tile_cols_ref, n_tiles)
    sign = 1.0 - 2.0 * where_ref[0].astype(F32)
    for p in range(n_tiles):
        spins_pm = (2 * field_ref[:, tile_ds(order[p], tile_len)] - 1).astype(F32)
        factor_ref[:, p * tile_len : (p + 1) * tile_len] = jnp.exp(sign * coupling * spins_pm)
    targets = []
    for z_ref, source_ref, tiles_in in zip(z_refs, sources, tiles_of):
        targets += [(z_ref, source_ref, slice(i * tile_len, (i + 1) * tile_len), tiles) for i, tiles in enumerate(tiles_in)]
    chain(n_tiles, tile_len, where_ref[2], factor_ref, weight_ref, targets)


def green_kernel(
    n_tiles, tile_len, own_tiles, tile_cols_ref, where_ref, mine_ref, theirs_ref, common_ref, last_ref,
    rows_ref, excess_ref, guess_ref, p_high_ref, p_low_ref, p_ref, c_ref, one8_ref, two8_ref, part8_ref, four8_ref,
):
    order = cycle_order(tile_cols_ref, n_tiles)
    matrix_order = mine_ref.shape[1]
    block = 2 * tile_len
    blocks = [slice(start, start + block) for start in range(0, matrix_order, block)]
    even = where_ref[2] == 0
    first, second = mine_ref[...], theirs_ref[...]
    pieces = [jnp.where(even, first, second), jnp.where(even, second, first)]
    for z_ref in (common_ref, last_ref):
        pieces += [z_ref[start : start + tile_len, :] for start in range(0, z_ref.shape[0], tile_len)]
    col_sum = sum(jnp.sum(piece, axis=0, keepdims=True) for piece in pieces)
    shrink = 0.5 / jnp.max(col_sum, axis=1, keepdims=True)
    for p, piece in enumerate(pieces):
        rows = slice(p * tile_len, (p + 1) * tile_len)
        p_ref[rows, :] = piece * shrink
        p_high_ref[rows, :] = p_ref[rows, :].astype(BF16)
    for rows in blocks:
        square = dot_by(p_high_ref[rows, :], p_high_ref[...], block)
        two8_ref[rows, :] = (square * 2.0**10).astype(F8)
        p_rows = p_ref[rows, :]
        p_low_ref[rows, :] = ((p_rows - p_high_ref[rows, :].astype(F32)) * 2.0**17).astype(F8)
        one8_ref[rows, :] = (p_rows * 2.0**9).astype(F8)
        c_ref[rows, :] = square - p_rows
    for rows in blocks:
        square = two8_ref[rows, :]
        cube = dot_by(square, one8_ref[...], block) * 2.0**-19
        part = c_ref[rows, :] - cube
        fourth = dot_by(square, two8_ref[...], block) * 2.0**-20
        c_ref[rows, :] = part + fourth
        part8_ref[rows, :] = (part * 2.0**8).astype(F8)
        four8_ref[rows, :] = (fourth * 2.0**12).astype(F8)
    for rows in blocks:
        guess = (-(c_ref[rows, :] + dot_by(part8_ref[rows, :], four8_ref[...], block) * 2.0**-20)).astype(BF16)
        guess_ref[rows, :] = guess
        excess_ref[rows, :] = guess.astype(F32) - p_ref[rows, :]

    own, _ = tiles_of_rows(where_ref, n_tiles, own_tiles)
    y = corrected([place_of(order, t) for t in own], tile_len, excess_ref, p_high_ref, p_low_ref, guess_ref)
    for q in range(n_tiles):
        rows_ref[:, tile_ds(order[q], tile_len)] = y[:, q * tile_len : (q + 1) * tile_len]


def rest_kernel(n_tiles, tile_len, own_tiles, tile_cols_ref, where_ref, excess_ref, guess_ref, p_high_ref, p_low_ref, out_ref, y_ref):
    order = cycle_order(tile_cols_ref, n_tiles)
    own, rest = tiles_of_rows(where_ref, n_tiles, own_tiles)
    y_ref[...] = corrected([place_of(order, t) for t in rest], tile_len, excess_ref, p_high_ref, p_low_ref, guess_ref)
    for i, t in enumerate(own):
        out_ref[:, i * tile_len : (i + 1) * tile_len] = y_ref[:, tile_ds(place_of(order, t), tile_len)]


def xcorr_kernel(n_tiles, tile_len, own_tiles, where_ref, rows_ref, rest_ref, other_ref, out_ref, block_ref, sems):
    own, rest = tiles_of_rows(where_ref, n_tiles, own_tiles)
    ids = (tile_len, tile_len)
    one = jnp.where(lax.broadcasted_iota(jnp.int32, ids, 0) == lax.broadcasted_iota(jnp.int32, ids, 1), 1.0, 0.0)
    copies = []
    for i, t in enumerate(own + rest):
        for j in range(own_tiles):
            cols = slice(j * tile_len, (j + 1) * tile_len)
            if i < own_tiles:
                green = -rows_ref[i * tile_len : (i + 1) * tile_len, tile_ds(own[j], tile_len)]
                if i == j:
                    green += one
            else:
                green = -rest_ref[(i - own_tiles) * tile_len : (i - own_tiles + 1) * tile_len, cols]
            block_ref[i, :, cols] = green * other_ref[cols, tile_ds(t, tile_len)].T
        copies.append(pltpu.make_async_copy(block_ref.at[i], out_ref.at[tile_ds(t, tile_len), :], sems.at[i]))
        copies[-1].start()
    for copy in copies:
        copy.wait()


def from_ahead(x, axis, by):
    size = lax.axis_size(axis)
    return lax.ppermute(x, axis, [((i + by) % size, i) for i in range(size)])


def gather_blocks(field, axis):
    size = lax.axis_size(axis)
    behind = from_ahead(field, axis, -1)
    held, by = jnp.concatenate([behind, field], axis=0), 2
    while by < size:
        held = jnp.concatenate([held, from_ahead(held, axis, by)], axis=0)
        by *= 2
    return behind, held[field.shape[0] :]


def per_device(ising_field, bond_sites, hopping, tile_cols):
    slices_here, matrix_order = ising_field.shape
    n_tiles = tile_cols.shape[0]
    tile_len = matrix_order // n_tiles
    pair_len = 2 * tile_len
    n_pairs = n_tiles // 2
    n_rows = lax.axis_size("rows")
    shared = 1
    while (n_tiles * shared) % n_rows:
        shared += 1
    own_tiles = n_tiles * shared // n_rows
    own_len = own_tiles * tile_len
    col_width = matrix_order // n_rows
    total_slices = slices_here * lax.axis_size("tm")
    coupling = 1.5 / math.sqrt(total_slices)
    smem = pl.BlockSpec(memory_space=pltpu.SMEM)
    vmem = pl.BlockSpec(memory_space=pltpu.VMEM)
    behind, ahead = gather_blocks(ising_field, "tm")
    cols_of_tiles = tile_cols.T
    weights = pl.pallas_call(
        functools.partial(kinetic_kernel, n_tiles, tile_len, 0.5 / total_slices),
        out_shape=jax.ShapeDtypeStruct((n_pairs, 4 * pair_len, pair_len), BF16),
        in_specs=[pl.BlockSpec(memory_space=pltpu.HBM)] * 3,
        out_specs=vmem,
        scratch_shapes=[
            pltpu.VMEM((n_pairs, pair_len, pair_len), F32),
            pltpu.SMEM(cols_of_tiles.shape, jnp.int32),
            pltpu.VMEM((2, hopping.shape[0]), jnp.int32),
            pltpu.VMEM((1, hopping.shape[0]), F32),
            pltpu.SemaphoreType.DMA((3,)),
        ],
        compiler_params=pltpu.CompilerParams(vmem_limit_bytes=24 * 2**20),
        cost_estimate=pl.CostEstimate(flops=4 * 10**9, bytes_accessed=4 * 10**6, transcendentals=0),
        name="kinetic",
    )(*[pltpu.with_memory_space_constraint(x, pltpu.HBM) for x in (cols_of_tiles, bond_sites.T, hopping[None, :])])
    where = jnp.stack([lax.axis_index("spin"), lax.axis_index("rows") // shared, lax.axis_index("rows") % 2]).astype(jnp.int32)
    square = (matrix_order, matrix_order)
    sizes = (n_tiles, tile_len, own_tiles)

    def chain_part(field, sources, *tiles_of):
        lengths = [len(tiles) * tile_len for tiles in tiles_of]
        return pl.pallas_call(
            functools.partial(chain_kernel, n_tiles, tile_len, coupling, tiles_of),
            out_shape=[jax.ShapeDtypeStruct((length, matrix_order), F32) for length in lengths],
            in_specs=[smem, smem] + [vmem] * (2 + len(sources)),
            out_specs=[vmem] * len(lengths),
            scratch_shapes=[pltpu.VMEM((field.shape[0], matrix_order), F32)],
            compiler_params=pltpu.CompilerParams(vmem_limit_bytes=24 * 2**20),
            cost_estimate=pl.CostEstimate(flops=25 * 10**5 * sum(lengths) * field.shape[0], bytes_accessed=4 * 10**6, transcendentals=0),
            name="chain",
        )(cols_of_tiles, where, field, weights, *sources)

    half = n_tiles // 2
    shared_tile, common_tiles, last_tiles = [(0, 1)], [(p,) for p in range(2, half)], [(p,) for p in range(half, n_tiles)]
    mine, common, last = chain_part(behind, [], shared_tile, common_tiles, last_tiles)
    mine, common = chain_part(ahead, [mine, common], shared_tile, common_tiles)
    theirs = lax.ppermute(mine, "rows", [(i, i ^ 1) for i in range(n_rows)])
    (last,) = chain_part(ahead, [last], last_tiles)
    rows, excess, guess, p_high, p_low = pl.pallas_call(
        functools.partial(green_kernel, *sizes),
        out_shape=[jax.ShapeDtypeStruct((own_len, matrix_order), F32), jax.ShapeDtypeStruct(square, F32)]
        + [jax.ShapeDtypeStruct(square, dtype) for dtype in (BF16, BF16, F8)],
        in_specs=[smem, smem] + [vmem] * 4,
        out_specs=[vmem] * 5,
        scratch_shapes=[pltpu.VMEM(square, F32)] * 2
        + [pltpu.VMEM(square, F8)] * 4,
        compiler_params=pltpu.CompilerParams(vmem_limit_bytes=32 * 2**20),
        cost_estimate=pl.CostEstimate(flops=5 * 10**9, bytes_accessed=6 * 10**6, transcendentals=0),
        name="green",
    )(cols_of_tiles, where, mine, theirs, common, last)
    size = lax.axis_size("spin")
    other_rows = lax.ppermute(rows, "spin", [(i, (i + 1) % size) for i in range(size)])
    rest = pl.pallas_call(
        functools.partial(rest_kernel, *sizes),
        out_shape=jax.ShapeDtypeStruct((matrix_order - own_len, own_len), F32),
        in_specs=[smem, smem, vmem, vmem, vmem, vmem],
        out_specs=vmem,
        scratch_shapes=[pltpu.VMEM((matrix_order - own_len, matrix_order), F32)],
        compiler_params=pltpu.CompilerParams(vmem_limit_bytes=24 * 2**20),
        cost_estimate=pl.CostEstimate(flops=2 * 10**9, bytes_accessed=4 * 10**6, transcendentals=0),
        name="rest",
    )(cols_of_tiles, where, excess, guess, p_high, p_low)
    xcorr = pl.pallas_call(
        functools.partial(xcorr_kernel, *sizes),
        out_shape=jax.ShapeDtypeStruct((matrix_order, own_len), F32),
        in_specs=[smem, vmem, vmem, vmem],
        out_specs=pl.BlockSpec(memory_space=pltpu.HBM),
        scratch_shapes=[pltpu.VMEM((n_tiles, tile_len, own_len), F32), pltpu.SemaphoreType.DMA((n_tiles,))],
        compiler_params=pltpu.CompilerParams(vmem_limit_bytes=16 * 2**20),
        name="xcorr",
    )(where, rows, rest, other_rows)
    if own_len != col_width:
        xcorr = lax.dynamic_slice_in_dim(xcorr, (lax.axis_index("rows") % shared) * col_width, col_width, 1)
    return xcorr[None, None]


def solution(mesh):
    placed = (P(("grp", "tm"), None), P(), P(), P())
    return jax.shard_map(
        per_device,
        mesh=mesh,
        in_specs=placed,
        out_specs=P("spin", ("grp", "tm"), None, "rows"),
        check_vma=False,
    )
```

```python
import functools
import math

import jax
import jax.numpy as jnp
from jax import lax
from jax.experimental import pallas as pl
from jax.experimental.pallas import tpu as pltpu
from jax.sharding import PartitionSpec as P

F32 = jnp.float32
BF16 = jnp.bfloat16
F8 = jnp.float8_e4m3fn


def dot(left, right):
    return jnp.dot(left, right, preferred_element_type=F32)


def dot_by(left, right, width):
    return jnp.concatenate([dot(left, right[:, at : at + width]) for at in range(0, right.shape[1], width)], axis=1)


def split(x):
    high = x.astype(BF16)
    return high, (x - high.astype(F32)).astype(BF16)


def cycle_order(tile_cols_ref, n_tiles):
    order = [jnp.int32(0), tile_cols_ref[1, 0]]
    while len(order) < n_tiles:
        before, here = order[-2], order[-1]
        one, two = tile_cols_ref[1, here], tile_cols_ref[2, here]
        order.append(jnp.where(one == before, two, one))
    return order


def place_of(order, tile):
    place = jnp.int32(0)
    for p in range(1, len(order)):
        place = jnp.where(order[p] == tile, p, place)
    return place


def tile_ds(tile, tile_len):
    return pl.ds(pl.multiple_of(tile * tile_len, tile_len), tile_len)


def kinetic_kernel(
    n_tiles, tile_len, scale, tile_cols_hbm, sites_hbm, hopping_hbm, weight_ref, acc_ref, tile_cols_ref, sites_ref, hopping_ref, sems
):
    copies = [
        pltpu.make_async_copy(source, target, sems.at[i])
        for i, (source, target) in enumerate(((tile_cols_hbm, tile_cols_ref), (sites_hbm, sites_ref), (hopping_hbm, hopping_ref)))
    ]
    for copy in copies:
        copy.start()
    acc_ref[...] = jnp.zeros_like(acc_ref)
    for copy in copies:
        copy.wait()
    order = cycle_order(tile_cols_ref, n_tiles)
    shift = tile_len.bit_length() - 1
    bonds = sites_ref.shape[1]
    pair_len = 2 * tile_len
    chunk = min(bonds, 1024)

    def position(site):
        tile = site >> shift
        place = jnp.zeros_like(site)
        for p in range(1, n_tiles):
            place = jnp.where(tile == order[p], p, place)
        return place, place * tile_len + (site & (tile_len - 1))

    def add_bonds(step):
        lanes = slice(step * chunk, (step + 1) * chunk)
        tile_a, site_a = position(sites_ref[0:1, lanes])
        tile_b, site_b = position(sites_ref[1:2, lanes])
        apart = jnp.abs(tile_a - tile_b)
        kept = (apart <= 1) | (apart == n_tiles - 1)
        weight = jnp.where(kept, hopping_ref[0:1, lanes] * scale, 0.0)
        weight_high = weight.astype(BF16).astype(F32)
        weight_low = weight - weight_high
        together = (tile_a >> 1) == (tile_b >> 1)
        swap = (tile_a != tile_b) & (together == ((tile_a & 1) == 1))
        first = jnp.where(swap, site_b, site_a)
        second = jnp.where(swap, site_a, site_b)
        slot = jnp.where(together, first, second - (second & (tile_len - 1)) + tile_len + (first & (tile_len - 1)))
        row_ids = lax.broadcasted_iota(jnp.int32, (tile_len, chunk), 0)
        high_of, low_of, ones_of = [], [], []
        for p in range(n_tiles):
            ids = row_ids + p * tile_len
            hit = slot == ids
            high_of.append(jnp.where(hit, weight_high, 0.0).astype(BF16))
            low_of.append(jnp.where(hit, weight_low, 0.0).astype(BF16))
            ones_of.append(jnp.where(second == ids, 1.0, 0.0).astype(BF16))
        for pair in range(n_tiles // 2):
            tiles = [2 * pair, 2 * pair + 1]
            left = jnp.concatenate([high_of[t] for t in tiles] + [low_of[t] for t in tiles], axis=0)
            right = jnp.concatenate([ones_of[2 * pair], ones_of[2 * pair + 1]], axis=0)
            both = lax.dot_general(left, right, (((1,), (1,)), ((), ())), preferred_element_type=F32)
            acc_ref[pair] += both[:pair_len] + both[pair_len:]

    for step in range(bonds // chunk):
        add_bonds(step)
    same = lax.broadcasted_iota(jnp.int32, (pair_len, pair_len), 0) == lax.broadcasted_iota(jnp.int32, (pair_len, pair_len), 1)
    zero = jnp.zeros((tile_len, tile_len), BF16)
    n_pairs = n_tiles // 2
    for pair in range(n_pairs):
        lower = acc_ref[pair, tile_len:, :]
        lower = jnp.concatenate([jnp.zeros((tile_len, tile_len), F32), lower[:, tile_len:]], axis=1)
        inner = jnp.concatenate([acc_ref[pair, :tile_len, :], lower], axis=0)
        high, low = split(inner + inner.T + jnp.where(same, 1.0, 0.0))
        weight_ref[pair, :pair_len, :] = high
        weight_ref[pair, pair_len : 2 * pair_len, :] = low
        above = acc_ref[pair, tile_len:, :tile_len]
        below = acc_ref[(pair + 1) % n_pairs, tile_len:, :tile_len].T
        for side, cell in enumerate((above, below)):
            high, low = split(cell)
            base = (2 + side) * pair_len
            weight_ref[pair, base : base + tile_len, :] = jnp.concatenate([high, low], axis=1)
            weight_ref[pair, base + tile_len : base + pair_len, :] = jnp.concatenate([high, zero], axis=1)


def chain(n_tiles, tile_len, parity, factor_ref, weight_ref, targets):
    slices, matrix_order = factor_ref.shape
    n_pairs = n_tiles // 2
    pair_len = 2 * tile_len

    def first_rows(p):
        row = factor_ref[slices - 1 : slices, p * tile_len : (p + 1) * tile_len]
        column = jnp.broadcast_to(row, (tile_len, tile_len)).T
        own = p // 2
        at = (p % 2) * tile_len
        whole = weight_ref[own, at : at + tile_len, :].astype(F32) + weight_ref[own, pair_len + at : pair_len + at + tile_len, :].astype(F32)
        if p % 2:
            into, base, next_tile = (own + 1) % n_pairs, 2 * pair_len, (p + 1) % n_tiles
        else:
            into, base, next_tile = (own - 1) % n_pairs, 3 * pair_len, (p - 1) % n_tiles
        cell = weight_ref[into, base : base + tile_len, :].astype(F32)
        cells = [jnp.zeros((tile_len, tile_len), F32)] * n_tiles
        cells[2 * own] = column * whole[:, :tile_len]
        cells[2 * own + 1] = column * whole[:, tile_len:]
        cells[next_tile] = column * (cell[:, :tile_len] + cell[:, tile_len:])
        return jnp.concatenate(cells, axis=1)

    started = targets[0][1] is not None
    for z_ref, _, rows, tiles in [] if started else targets:
        z_ref[rows, :] = first_rows(tiles[0]) if len(tiles) == 1 else jnp.where(parity == 0, first_rows(tiles[0]), first_rows(tiles[1]))

    def tile(x, t):
        t = t % n_tiles
        return x[:, t * tile_len : (t + 1) * tile_len]

    def one_slice(index, reach, afresh=False):
        factor = factor_ref[pl.ds(index, 1), :]
        for z_ref, source_ref, rows, tiles in targets:
            high, low = split((source_ref if afresh else z_ref)[rows, :] * factor)

            def live(t):
                return any(min((t - p) % n_tiles, (p - t) % n_tiles) <= reach for p in tiles)

            for pair in range(n_pairs):
                lanes = slice(pair * pair_len, (pair + 1) * pair_len)
                weight = weight_ref[pair]
                inner = None
                if live(2 * pair) or live(2 * pair + 1):
                    inner = dot(
                        jnp.concatenate([high[:, lanes], low[:, lanes], high[:, lanes]], axis=1),
                        jnp.concatenate([weight[:pair_len], weight[:pair_len], weight[pair_len : 2 * pair_len]], axis=0),
                    )
                for side, t in enumerate((2 * pair - 1, 2 * pair + 2)):
                    parts = [] if inner is None else [inner[:, side * tile_len : (side + 1) * tile_len]]
                    if live(t):
                        base = (2 + side) * pair_len
                        part = dot(jnp.concatenate([tile(high, t), tile(low, t)], axis=1), weight[base : base + pair_len])
                        parts.append(part[:, :tile_len] + part[:, tile_len:])
                    to = (2 * pair + side) * tile_len
                    z_ref[rows, to : to + tile_len] = sum(parts) if parts else jnp.zeros((tile_len, tile_len), F32)

    steps = slices if started else slices - 1
    peeled = steps if steps <= 16 else n_tiles // 2
    for step in range(peeled):
        one_slice(steps - 1 - step, n_tiles if started else step + 1, started and step == 0)
    if peeled < steps:
        lax.fori_loop(peeled, steps, lambda step, carry: (one_slice(steps - 1 - step, n_tiles), carry)[1], 0)


def corrected(places, tile_len, excess_ref, p_high_ref, p_low_ref, guess_ref):
    def rows_of(ref):
        return jnp.concatenate([ref[tile_ds(p, tile_len), :] for p in places], axis=0)

    guess = rows_of(guess_ref)
    guess8 = (guess.astype(F32) * 2.0**8).astype(F8)
    small = dot_by(guess8, p_low_ref[...], 2 * tile_len) * 2.0**-25
    residual = rows_of(excess_ref) + dot_by(guess, p_high_ref[...], 2 * tile_len) + small
    return (guess.astype(F32) - residual) + dot_by(residual.astype(BF16), guess_ref[...], 2 * tile_len)


def tiles_of_rows(where_ref, n_tiles, own_tiles):
    first = where_ref[1] * own_tiles
    own = [first + i for i in range(own_tiles)]
    rest = [jnp.where(first <= i, i + own_tiles, i) for i in range(n_tiles - own_tiles)]
    return own, rest


def chain_kernel(n_tiles, tile_len, coupling, tiles_of, tile_cols_ref, where_ref, field_ref, weight_ref, *refs):
    *z_refs, factor_ref = refs
    parts = len(tiles_of)
    sources, z_refs = (z_refs[:-parts] or [None] * parts), z_refs[-parts:]
    order = cycle_order(tile_cols_ref, n_tiles)
    sign = 1.0 - 2.0 * where_ref[0].astype(F32)
    for p in range(n_tiles):
        spins_pm = (2 * field_ref[:, tile_ds(order[p], tile_len)] - 1).astype(F32)
        factor_ref[:, p * tile_len : (p + 1) * tile_len] = jnp.exp(sign * coupling * spins_pm)
    targets = []
    for z_ref, source_ref, tiles_in in zip(z_refs, sources, tiles_of):
        targets += [(z_ref, source_ref, slice(i * tile_len, (i + 1) * tile_len), tiles) for i, tiles in enumerate(tiles_in)]
    chain(n_tiles, tile_len, where_ref[2], factor_ref, weight_ref, targets)


def green_kernel(
    n_tiles, tile_len, own_tiles, tile_cols_ref, where_ref, mine_ref, theirs_ref, common_ref, last_ref,
    rows_ref, excess_ref, guess_ref, p_high_ref, p_low_ref, p_ref, c_ref, one8_ref, two8_ref, part8_ref, four8_ref,
):
    order = cycle_order(tile_cols_ref, n_tiles)
    matrix_order = mine_ref.shape[1]
    block = 2 * tile_len
    blocks = [slice(start, start + block) for start in range(0, matrix_order, block)]
    even = where_ref[2] == 0
    first, second = mine_ref[...], theirs_ref[...]
    pieces = [jnp.where(even, first, second), jnp.where(even, second, first)]
    for z_ref in (common_ref, last_ref):
        pieces += [z_ref[start : start + tile_len, :] for start in range(0, z_ref.shape[0], tile_len)]
    col_sum = sum(jnp.sum(piece, axis=0, keepdims=True) for piece in pieces)
    shrink = 0.5 / jnp.max(col_sum, axis=1, keepdims=True)
    for p, piece in enumerate(pieces):
        rows = slice(p * tile_len, (p + 1) * tile_len)
        p_ref[rows, :] = piece * shrink
        p_high_ref[rows, :] = p_ref[rows, :].astype(BF16)
    for rows in blocks:
        square = dot_by(p_high_ref[rows, :], p_high_ref[...], block)
        two8_ref[rows, :] = (square * 2.0**10).astype(F8)
        p_rows = p_ref[rows, :]
        p_low_ref[rows, :] = ((p_rows - p_high_ref[rows, :].astype(F32)) * 2.0**17).astype(F8)
        one8_ref[rows, :] = (p_rows * 2.0**9).astype(F8)
        c_ref[rows, :] = square - p_rows
    for rows in blocks:
        square = two8_ref[rows, :]
        cube = dot_by(square, one8_ref[...], block) * 2.0**-19
        part = c_ref[rows, :] - cube
        fourth = dot_by(square, two8_ref[...], block) * 2.0**-20
        c_ref[rows, :] = part + fourth
        part8_ref[rows, :] = (part * 2.0**8).astype(F8)
        four8_ref[rows, :] = (fourth * 2.0**12).astype(F8)
    for rows in blocks:
        guess = (-(c_ref[rows, :] + dot_by(part8_ref[rows, :], four8_ref[...], block) * 2.0**-20)).astype(BF16)
        guess_ref[rows, :] = guess
        excess_ref[rows, :] = guess.astype(F32) - p_ref[rows, :]

    own, _ = tiles_of_rows(where_ref, n_tiles, own_tiles)
    y = corrected([place_of(order, t) for t in own], tile_len, excess_ref, p_high_ref, p_low_ref, guess_ref)
    for q in range(n_tiles):
        rows_ref[:, tile_ds(order[q], tile_len)] = y[:, q * tile_len : (q + 1) * tile_len]


def rest_kernel(n_tiles, tile_len, own_tiles, tile_cols_ref, where_ref, excess_ref, guess_ref, p_high_ref, p_low_ref, out_ref, y_ref):
    order = cycle_order(tile_cols_ref, n_tiles)
    own, rest = tiles_of_rows(where_ref, n_tiles, own_tiles)
    y_ref[...] = corrected([place_of(order, t) for t in rest], tile_len, excess_ref, p_high_ref, p_low_ref, guess_ref)
    for i, t in enumerate(own):
        out_ref[:, i * tile_len : (i + 1) * tile_len] = y_ref[:, tile_ds(place_of(order, t), tile_len)]


def xcorr_kernel(n_tiles, tile_len, own_tiles, where_ref, rows_ref, rest_ref, other_ref, out_ref, block_ref, sems):
    own, rest = tiles_of_rows(where_ref, n_tiles, own_tiles)
    ids = (tile_len, tile_len)
    one = jnp.where(lax.broadcasted_iota(jnp.int32, ids, 0) == lax.broadcasted_iota(jnp.int32, ids, 1), 1.0, 0.0)
    copies = []
    for i, t in enumerate(own + rest):
        for j in range(own_tiles):
            cols = slice(j * tile_len, (j + 1) * tile_len)
            if i < own_tiles:
                green = -rows_ref[i * tile_len : (i + 1) * tile_len, tile_ds(own[j], tile_len)]
                if i == j:
                    green += one
            else:
                green = -rest_ref[(i - own_tiles) * tile_len : (i - own_tiles + 1) * tile_len, cols]
            block_ref[i, :, cols] = green * other_ref[cols, tile_ds(t, tile_len)].T
        copies.append(pltpu.make_async_copy(block_ref.at[i], out_ref.at[tile_ds(t, tile_len), :], sems.at[i]))
        copies[-1].start()
    for copy in copies:
        copy.wait()


def from_ahead(x, axis, by):
    size = lax.axis_size(axis)
    return lax.ppermute(x, axis, [((i + by) % size, i) for i in range(size)])


def gather_blocks(field, axis):
    size = lax.axis_size(axis)
    behind = from_ahead(field, axis, -1)
    held, by = jnp.concatenate([behind, field], axis=0), 2
    while by < size:
        held = jnp.concatenate([held, from_ahead(held, axis, by)], axis=0)
        by *= 2
    return behind, held[field.shape[0] :]


def per_device(ising_field, bond_sites, hopping, tile_cols):
    slices_here, matrix_order = ising_field.shape
    n_tiles = tile_cols.shape[0]
    tile_len = matrix_order // n_tiles
    pair_len = 2 * tile_len
    n_pairs = n_tiles // 2
    n_rows = lax.axis_size("rows")
    shared = 1
    while (n_tiles * shared) % n_rows:
        shared += 1
    own_tiles = n_tiles * shared // n_rows
    own_len = own_tiles * tile_len
    col_width = matrix_order // n_rows
    total_slices = slices_here * lax.axis_size("tm")
    coupling = 1.5 / math.sqrt(total_slices)
    smem = pl.BlockSpec(memory_space=pltpu.SMEM)
    vmem = pl.BlockSpec(memory_space=pltpu.VMEM)
    behind, ahead = gather_blocks(ising_field, "tm")
    cols_of_tiles = tile_cols.T
    weights = pl.pallas_call(
        functools.partial(kinetic_kernel, n_tiles, tile_len, 0.5 / total_slices),
        out_shape=jax.ShapeDtypeStruct((n_pairs, 4 * pair_len, pair_len), BF16),
        in_specs=[pl.BlockSpec(memory_space=pltpu.HBM)] * 3,
        out_specs=vmem,
        scratch_shapes=[
            pltpu.VMEM((n_pairs, pair_len, pair_len), F32),
            pltpu.SMEM(cols_of_tiles.shape, jnp.int32),
            pltpu.VMEM((2, hopping.shape[0]), jnp.int32),
            pltpu.VMEM((1, hopping.shape[0]), F32),
            pltpu.SemaphoreType.DMA((3,)),
        ],
        compiler_params=pltpu.CompilerParams(vmem_limit_bytes=24 * 2**20),
        cost_estimate=pl.CostEstimate(flops=4 * 10**9, bytes_accessed=4 * 10**6, transcendentals=0),
        name="kinetic",
    )(*[pltpu.with_memory_space_constraint(x, pltpu.HBM) for x in (cols_of_tiles, bond_sites.T, hopping[None, :])])
    where = jnp.stack([lax.axis_index("spin"), lax.axis_index("rows") // shared, lax.axis_index("rows") % 2]).astype(jnp.int32)
    square = (matrix_order, matrix_order)
    sizes = (n_tiles, tile_len, own_tiles)

    def chain_part(field, sources, *tiles_of):
        lengths = [len(tiles) * tile_len for tiles in tiles_of]
        return pl.pallas_call(
            functools.partial(chain_kernel, n_tiles, tile_len, coupling, tiles_of),
            out_shape=[jax.ShapeDtypeStruct((length, matrix_order), F32) for length in lengths],
            in_specs=[smem, smem] + [vmem] * (2 + len(sources)),
            out_specs=[vmem] * len(lengths),
            scratch_shapes=[pltpu.VMEM((field.shape[0], matrix_order), F32)],
            compiler_params=pltpu.CompilerParams(vmem_limit_bytes=24 * 2**20),
            cost_estimate=pl.CostEstimate(flops=25 * 10**5 * sum(lengths) * field.shape[0], bytes_accessed=4 * 10**6, transcendentals=0),
            name="chain",
        )(cols_of_tiles, where, field, weights, *sources)

    half = n_tiles // 2
    shared_tile, common_tiles, last_tiles = [(0, 1)], [(p,) for p in range(2, half)], [(p,) for p in range(half, n_tiles)]
    mine, common, last = chain_part(behind, [], shared_tile, common_tiles, last_tiles)
    mine, common = chain_part(ahead, [mine, common], shared_tile, common_tiles)
    theirs = lax.ppermute(mine, "rows", [(i, i ^ 1) for i in range(n_rows)])
    (last,) = chain_part(ahead, [last], last_tiles)
    rows, excess, guess, p_high, p_low = pl.pallas_call(
        functools.partial(green_kernel, *sizes),
        out_shape=[jax.ShapeDtypeStruct((own_len, matrix_order), F32), jax.ShapeDtypeStruct(square, F32)]
        + [jax.ShapeDtypeStruct(square, dtype) for dtype in (BF16, BF16, F8)],
        in_specs=[smem, smem] + [vmem] * 4,
        out_specs=[vmem] * 5,
        scratch_shapes=[pltpu.VMEM(square, F32)] * 2
        + [pltpu.VMEM(square, F8)] * 4,
        compiler_params=pltpu.CompilerParams(vmem_limit_bytes=32 * 2**20),
        cost_estimate=pl.CostEstimate(flops=5 * 10**9, bytes_accessed=6 * 10**6, transcendentals=0),
        name="green",
    )(cols_of_tiles, where, mine, theirs, common, last)
    size = lax.axis_size("spin")
    other_rows = lax.ppermute(rows, "spin", [(i, (i + 1) % size) for i in range(size)])
    rest = pl.pallas_call(
        functools.partial(rest_kernel, *sizes),
        out_shape=jax.ShapeDtypeStruct((matrix_order - own_len, own_len), F32),
        in_specs=[smem, smem, vmem, vmem, vmem, vmem],
        out_specs=vmem,
        scratch_shapes=[pltpu.VMEM((matrix_order - own_len, matrix_order), F32)],
        compiler_params=pltpu.CompilerParams(vmem_limit_bytes=24 * 2**20),
        cost_estimate=pl.CostEstimate(flops=2 * 10**9, bytes_accessed=4 * 10**6, transcendentals=0),
        name="rest",
    )(cols_of_tiles, where, excess, guess, p_high, p_low)
    xcorr = pl.pallas_call(
        functools.partial(xcorr_kernel, *sizes),
        out_shape=jax.ShapeDtypeStruct((matrix_order, own_len), F32),
        in_specs=[smem, vmem, vmem, vmem],
        out_specs=pl.BlockSpec(memory_space=pltpu.HBM),
        scratch_shapes=[pltpu.VMEM((n_tiles, tile_len, own_len), F32), pltpu.SemaphoreType.DMA((n_tiles,))],
        compiler_params=pltpu.CompilerParams(vmem_limit_bytes=16 * 2**20),
        name="xcorr",
    )(where, rows, rest, other_rows)
    if own_len != col_width:
        xcorr = lax.dynamic_slice_in_dim(xcorr, (lax.axis_index("rows") % shared) * col_width, col_width, 1)
    return xcorr[None, None]


def solution(mesh):
    placed = (P(("grp", "tm"), None), P(), P(), P())
    return jax.shard_map(
        per_device,
        mesh=mesh,
        in_specs=placed,
        out_specs=P("spin", ("grp", "tm"), None, "rows"),
        check_vma=False,
    )
```
